32 devices in a mesh: seq: 4 (over y, core), dp: 8 (over z, x).
Axes of the slice: x: 2, y: 2, z: 4, core: 2. Of those that a mesh axis runs over, the one named last changes fastest.
Arguments:
- mlp_hidden: bfloat16 [8, 256, 8192], P('dp', None, 'seq'), may hold values from -6 to 6
- encoder_stream: bfloat16 [8, 256, 4096], P('dp', 'seq'), may hold values from -18 to 18
- down_proj: bfloat16 [8192, 4096], P('seq', 'dp'), may hold values from -0.0625 to 0.0625
- final_gain: bfloat16 [4096], replicated, may hold values from 0.25 to 1.75
- kv_proj: bfloat16 [4096, 2, 2048], P('dp', None, 'seq'), may hold values from -0.09375 to 0.09375
- queries: bfloat16 [8, 128, 2048], P('dp', None, 'seq'), may hold values from -640 to 640
- out_proj: bfloat16 [2048, 4096], P('seq'), may hold values from -0.39648438 to 0.39648438
- enc_len: int32 [8], P('dp'), may hold values from 128 to 256, as said below
- dec_pad: int32 [8], P('dp'), may hold values from 0 to 64, as said below
Outputs:
- cross_out: bfloat16 [8, 128, 4096], P('dp', 'seq')
The draws below stay inside these ranges and needn't reach their ends.
Inputs may be any that keep to these rules, and one draw needn't show every extreme that they name: `enc_len`: at least one filing uses all 256 positions and one uses 256 // 2. `dec_pad`: some filing has no padding and some has 64 padded rows.
All inputs are finite; a program needn't handle non-finite values.
Results may differ from the reference program's by a relative error of at most 0.015.
The reference program's roundings to bfloat16 on the way (of `encoded`, `key_value`, `attn` and `attended`) count: a program that leaves them out, or rounds other values in their place, can miss the bound.
Values may be sent and summed in bfloat16 or wider, within the bound.
No kernel may reach another device: no remote copies, remote signals or barrier semaphores. Data moves between devices by JAX's collectives and lax.ppermute only.
A program may use at most 128 MiB of HBM per device.

```python
import math
import jax
import jax.numpy as jnp
from jax import lax

D = 4096
HD = 256
HEADS = 8
FF = 8192
DEC = 128
ENC = 256
FILINGS = 8


def draw_encoder_stream(key, part):
    key_base, key_row, key_col = jax.random.split(key, 3)
    row_scale = jnp.exp(jax.random.uniform(key_row, (FILINGS, ENC, 1), jnp.float32, -1.2, 1.2))
    col_scale = jnp.exp(jax.random.uniform(key_col, (1, 1, D), jnp.float32, -1.2, 1.2))
    normal_part = jnp.clip(jax.random.normal(key_base, (FILINGS, ENC, D), jnp.float32), -4.0, 4.0)
    return (0.4 * normal_part * row_scale * col_scale).astype(jnp.bfloat16)


def draw_queries(key, part):
    key_base = jax.random.fold_in(key, 0)
    normal_part = 2.5 * jnp.clip(jax.random.normal(key_base, (FILINGS, DEC, HEADS * HD), jnp.float32), -4.0, 4.0)
    return normal_part.astype(jnp.bfloat16)


def draw_enc_len(key, part):
    key_draw, key_pick = jax.random.split(jax.random.fold_in(key, 11), 2)
    drawn = jax.random.randint(key_draw, (FILINGS,), ENC // 2, ENC + 1)
    chosen = jax.random.permutation(key_pick, FILINGS)
    drawn = drawn.at[chosen[0]].set(ENC).at[chosen[1]].set(ENC // 2)
    return drawn.astype(jnp.int32)


def draw_dec_pad(key, part):
    key_draw, key_pick = jax.random.split(jax.random.fold_in(key, 23), 2)
    drawn = jax.random.randint(key_draw, (FILINGS,), 0, DEC // 2 + 1)
    chosen = jax.random.permutation(key_pick, FILINGS)
    drawn = drawn.at[chosen[0]].set(0).at[chosen[1]].set(DEC // 2)
    return drawn.astype(jnp.int32)


def levels(rng, dims, cuts, low, high):
    factor_of = 1.0
    for axis_at, shards_of in cuts:
        steps = jax.random.uniform(jax.random.fold_in(jax.random.fold_in(rng, 6), axis_at), (shards_of,), jnp.float32, low / len(cuts), high / len(cuts))
        factor_of = factor_of * jnp.repeat(jnp.exp(steps), dims[axis_at] // shards_of).reshape((-1,) + (1,) * (len(dims) - 1 - axis_at))
    return factor_of


def centred(key, extent, scale, reach, pieces=(), kind=jnp.bfloat16):
    values = jax.random.normal(key, extent, jnp.float32) * scale
    if len(pieces) > 0:
        values = levels(key, extent, pieces, -0.22, 0.18) * values
    return jnp.clip(values, min=-reach, max=reach).astype(kind)


def setup_inputs(seed: int = 0) -> dict:
    key_list = jax.random.split(jax.random.key(seed), 10)
    mlp_hidden = centred(key_list[0], (FILINGS, ENC, FF), 1.0, 6.0, ((0, 8), (2, 4)))
    encoder_stream = draw_encoder_stream(jax.random.fold_in(key_list[9], 71), 0)
    down_proj = centred(key_list[2], (FF, D), FF ** -0.5, 0.0625, ((0, 4), (1, 8)))
    final_gain = jnp.clip(1.0 + 0.15 * jax.random.normal(key_list[3], (D,), jnp.float32), 0.25, 1.75).astype(jnp.bfloat16)
    kv_proj = centred(key_list[4], (D, 2, HEADS * HD), D ** -0.5, 0.09375, ((0, 8), (2, 4)))
    queries = draw_queries(jax.random.fold_in(key_list[9], 71), 0)
    out_proj = centred(key_list[6], (HEADS * HD, D), (3.0 * (HEADS * HD) ** -0.5), 0.39648438, ((0, 4),))
    enc_len = draw_enc_len(jax.random.fold_in(key_list[9], 71), 0)
    dec_pad = draw_dec_pad(jax.random.fold_in(key_list[9], 71), 0)
    return {"mlp_hidden": mlp_hidden, "encoder_stream": encoder_stream, "down_proj": down_proj, "final_gain": final_gain, "kv_proj": kv_proj, "queries": queries, "out_proj": out_proj, "enc_len": enc_len, "dec_pad": dec_pad}


def one_filing(filing_hidden, filing_stream, filing_query, filing_len, filing_pad, down_proj, final_gain, kv_proj, out_proj):
    mlp_out = jnp.dot(filing_hidden, down_proj, preferred_element_type=jnp.float32)
    resid = filing_stream.astype(jnp.float32) + mlp_out
    spread = lax.optimization_barrier(jnp.mean(resid * resid, axis=-1, keepdims=True))
    encoded = (resid * lax.rsqrt(spread + 1e-06) * final_gain.astype(jnp.float32)).astype(jnp.bfloat16)
    key_value = jnp.dot(encoded, kv_proj.reshape(D, 2 * HEADS * HD), preferred_element_type=jnp.float32).astype(jnp.bfloat16)
    key_value = key_value.reshape(ENC, 2, HEADS, HD)
    key_rows = key_value[:, 0].astype(jnp.float32)
    value_rows = key_value[:, 1].astype(jnp.float32)
    query_rows = filing_query.reshape(DEC, HEADS, HD).astype(jnp.float32)
    scores = jnp.einsum('qhd,khd->hqk', query_rows, key_rows) / math.sqrt(HD)
    visible = jnp.arange(ENC) < filing_len
    scores = jnp.where(visible[None, None, :], scores, -jnp.inf)
    highest = lax.optimization_barrier(jnp.max(scores, axis=-1, keepdims=True))
    expo = jnp.exp(scores - highest)
    attn = (expo / lax.optimization_barrier(jnp.sum(expo, axis=-1, keepdims=True))).astype(jnp.bfloat16)
    attended = jnp.einsum('hqk,khd->qhd', attn.astype(jnp.float32), value_rows).astype(jnp.bfloat16)
    row_live = jnp.arange(DEC) < DEC - filing_pad
    attended = jnp.where(row_live[:, None, None], attended, jnp.zeros_like(attended)).reshape(DEC, HEADS * HD)
    summed = jnp.dot(attended, out_proj, preferred_element_type=jnp.float32)
    return summed.astype(jnp.bfloat16)

def reference(mlp_hidden, encoder_stream, down_proj, final_gain, kv_proj, queries, out_proj, enc_len, dec_pad):

    def per_filing(items):
        return one_filing(items[0], items[1], items[2], items[3], items[4], down_proj, final_gain, kv_proj, out_proj)
    return lax.map(per_filing, (mlp_hidden, encoder_stream, queries, enc_len, dec_pad))
```

```python
import math

import jax
import jax.numpy as jnp
from jax import lax
from jax.sharding import PartitionSpec as P

HD = 256


class Line:
    def __init__(self, name, total, size, stride):
        self.name, self.total, self.size, self.stride = name, total, size, stride
        self.at = (lax.axis_index(name) // stride) % size

    def place(self, index):
        return (index // self.stride) % self.size

    def shift(self, value, step):
        pairs = [
            (i, i + step * self.stride)
            for i in range(self.total)
            if 0 <= self.place(i) + step < self.size
        ]
        return lax.ppermute(value, self.name, pairs)

    def swap(self, value, mask):
        pairs = [
            (i, i + ((self.place(i) ^ mask) - self.place(i)) * self.stride)
            for i in range(self.total)
        ]
        return lax.ppermute(value, self.name, pairs)

    def gather(self, pieces):
        n = self.size
        if n == 1:
            return [pieces]
        if n == 2:
            return [pieces, [self.swap(p, 1) for p in pieces]]
        hops = {}
        up = down = pieces
        for step in range(1, n):
            up = [self.shift(p, 1) for p in up]
            down = [self.shift(p, -1) for p in down]
            hops[step], hops[-step] = up, down
        slots = [pieces]
        for m in range(1, n):
            moves = sorted({i - (i ^ m) for i in range(n)})
            slot = []
            for p in range(len(pieces)):
                value = hops[moves[0]][p]
                for move in moves[1:]:
                    value = jnp.where(self.at - (self.at ^ m) == move, hops[move][p], value)
                slot.append(value)
            slots.append(slot)
        return slots


def after(values, earlier):
    out = lax.optimization_barrier((tuple(values), tuple(earlier)))
    return list(out[0])


def on_device(
    mlp_hidden, encoder_stream, down_proj, final_gain, kv_proj, queries, out_proj, enc_len, dec_pad
):
    seq, dp = lax.axis_size("seq"), lax.axis_size("dp")
    nx = 1 << ((dp.bit_length() - 1) // 2)
    nz = dp // nx
    nc = 2
    ny = seq // nc
    z = Line("dp", dp, nz, nx)
    x = Line("dp", dp, nx, 1)
    y = Line("seq", seq, ny, nc)
    c = Line("seq", seq, nc, 1)

    hidden = mlp_hidden[0]
    enc_total, depth = hidden.shape
    rows = enc_total // seq
    block = down_proj.shape[1]
    width = block * dp
    dot = lambda a, b: jnp.dot(a, b, preferred_element_type=jnp.float32)

    halves = [hidden[: enc_total // 2], hidden[enc_total // 2 :]]
    hidden_slots = z.gather(halves)
    down_slots = [s[0] for s in x.gather([down_proj])]

    keys_local, values_local = kv_proj[:, 0], kv_proj[:, 1]
    kv_own = after([keys_local, values_local], hidden_slots[-1])
    kv_z = z.gather(kv_own)
    kv_slots = [x.gather(slot) for slot in kv_z]

    summed = []
    for m in range(nz):
        a = jnp.concatenate(hidden_slots[m], axis=0).reshape(ny, nc, rows, depth)
        pick = lambda i: lax.dynamic_index_in_dim(a, i, 1, keepdims=False).reshape(ny * rows, depth)
        product = lambda i: jnp.concatenate([dot(pick(i), w) for w in down_slots], axis=1)
        part = product(c.at) + c.swap(product(1 - c.at), 1)
        part = part.reshape(ny, rows, nx * block)
        total = lax.dynamic_index_in_dim(part, y.at, 0, keepdims=False)
        for k in range(1, ny):
            other = lax.dynamic_index_in_dim(part, y.at ^ k, 0, keepdims=False)
            total = total + y.swap(other, k)
        summed.append(total if m == 0 else z.swap(total, m))

    stream = encoder_stream[0]
    gain = final_gain.astype(jnp.float32)
    resid, gains = [], []
    for m in range(nz):
        for k in range(nx):
            start = ((z.at ^ m) * nx + (x.at ^ k)) * block
            piece = lax.dynamic_slice_in_dim(stream, start, block, 1).astype(jnp.float32)
            resid.append(piece + summed[m][:, k * block : (k + 1) * block])
            gains.append(lax.dynamic_slice_in_dim(gain, start, block, 0))
    resid = jnp.concatenate(resid, axis=1)
    gains = jnp.concatenate(gains, axis=0)
    spread = jnp.sum(resid * resid, axis=-1, keepdims=True) / width
    normed = (resid * lax.rsqrt(spread + 1e-06) * gains).astype(jnp.bfloat16)
    encoded, places = [], []
    for k, (far,) in enumerate(y.gather([normed])):
        encoded += [far, c.swap(far, 1)]
        for j in range(nc):
            start = ((y.at ^ k) * nc + (c.at ^ j)) * rows
            places.append(start + jnp.arange(rows, dtype=jnp.int32))
    encoded = jnp.concatenate(encoded, axis=0)
    visible = jnp.concatenate(places) < enc_len[0]

    keys = values = None
    for m in range(nz):
        for k in range(nx):
            at = (m * nx + k) * block
            piece = encoded[:, at : at + block]
            wk, wv = kv_slots[m][k]
            dk, dv = dot(piece, wk), dot(piece, wv)
            keys = dk if keys is None else keys + dk
            values = dv if values is None else values + dv
    keys = keys.astype(jnp.bfloat16)
    values = values.astype(jnp.bfloat16)

    heads_here = queries.shape[2] // HD
    dec_rows = queries.shape[1]
    attended = []
    for h in range(heads_here):
        cols = slice(h * HD, (h + 1) * HD)
        scores = lax.dot_general(
            queries[0][:, cols], keys[:, cols], (((1,), (1,)), ((), ())),
            preferred_element_type=jnp.float32,
        ) / math.sqrt(HD)
        scores = jnp.where(visible[None, :], scores, -jnp.inf)
        expo = jnp.exp(scores - jnp.max(scores, axis=-1, keepdims=True))
        attention = (expo / jnp.sum(expo, axis=-1, keepdims=True)).astype(jnp.bfloat16)
        attended.append(dot(attention, values[:, cols]).astype(jnp.bfloat16))
    attended = jnp.concatenate(attended, axis=1)
    row_live = jnp.arange(dec_rows, dtype=jnp.int32) < dec_rows - dec_pad[0]
    attended = jnp.where(row_live[:, None], attended, jnp.zeros_like(attended))

    out_rows = dec_rows // seq
    att = attended.reshape(ny, nc, out_rows, heads_here * HD)
    pick = lambda i: lax.dynamic_index_in_dim(att, i, 1, keepdims=False).reshape(
        ny * out_rows, heads_here * HD
    )
    part = dot(pick(c.at), out_proj) + c.swap(dot(pick(1 - c.at), out_proj), 1)
    part = part.reshape(ny, out_rows, width)
    total = lax.dynamic_index_in_dim(part, y.at, 0, keepdims=False)
    for k in range(1, ny):
        total = total + y.swap(lax.dynamic_index_in_dim(part, y.at ^ k, 0, keepdims=False), k)
    return total.astype(jnp.bfloat16)[None]


def solution(mesh):
    placed = (
        P("dp", None, "seq"),
        P("dp", "seq", None),
        P("seq", "dp"),
        P(),
        P("dp", None, "seq"),
        P("dp", None, "seq"),
        P("seq", None),
        P("dp"),
        P("dp"),
    )
    return jax.shard_map(
        on_device, mesh=mesh, in_specs=placed, out_specs=P("dp", "seq", None), check_vma=False
    )
```

```python
import math

import jax
import jax.numpy as jnp
from jax import lax
from jax.sharding import PartitionSpec as P

HD = 256


class Line:
    def __init__(self, name, total, size, stride):
        self.name, self.total, self.size, self.stride = name, total, size, stride
        self.at = (lax.axis_index(name) // stride) % size

    def place(self, index):
        return (index // self.stride) % self.size

    def shift(self, value, step):
        pairs = [
            (i, i + step * self.stride)
            for i in range(self.total)
            if 0 <= self.place(i) + step < self.size
        ]
        return lax.ppermute(value, self.name, pairs)

    def swap(self, value, mask):
        pairs = [
            (i, i + ((self.place(i) ^ mask) - self.place(i)) * self.stride)
            for i in range(self.total)
        ]
        return lax.ppermute(value, self.name, pairs)

    def cross(self, value):
        turned = {1: 2, 2: 1}
        pairs = [
            (i, i + (turned.get(self.place(i), self.place(i)) - self.place(i)) * self.stride)
            for i in range(self.total)
        ]
        return lax.ppermute(value, self.name, pairs)

    def gather(self, pieces, gates=((), ())):
        n = self.size
        if n != 4:
            return [pieces] + [[self.swap(p, m) for p in pieces] for m in range(1, n)]
        inner = (self.at == 1) | (self.at == 2)
        first = after(pieces, gates[0])
        middle = after(pieces, gates[1])
        slots = [pieces, [], [], []]
        for p, q in zip(first, middle):
            near = self.swap(p, 1)
            far = self.cross(q)
            far2 = self.cross(near)
            out2 = self.swap(far, 1)
            out3 = self.swap(far2, 1)
            slots[1].append(near)
            slots[2].append(jnp.where(inner, far2, out2))
            slots[3].append(jnp.where(inner, far, out3))
        return slots


def after(values, earlier):
    if not earlier:
        return list(values)
    out = lax.optimization_barrier((tuple(values), tuple(earlier)))
    return list(out[0])


def tick(*groups):
    sizes = [len(g) for g in groups]
    flat = lax.optimization_barrier(tuple(v for g in groups for v in g))
    out, at = [], 0
    for size in sizes:
        out.append(list(flat[at : at + size]))
        at += size
    return out


def woven(z, x, halves, downs, kv, dot, seq_core, seq_y):
    E, O, X = (lambda v: z.swap(v, 1)), z.cross, (lambda v: x.swap(v, 1))
    inner = (z.at == 1) | (z.at == 2)
    choose = lambda a, b: jnp.where(inner, a, b)
    (ha, hb), (da, db), (k, v) = halves, downs, kv

    e1a, o1a, xda = E(ha), O(ha), X(da)
    e1b, o1b, xdb = E(hb), O(hb), X(db)
    e2a, o2a = E(o1a), O(e1a)
    e2b, o2b = E(o1b), O(e1b)
    (e2a, o2a, xda), (k, v) = tick((e2a, o2a, xda), (k, v))
    e3a = E(o2a)
    o1k = O(k)
    wa = jnp.concatenate([da, xda], axis=1)
    c0, c1 = dot(ha, wa), dot(e1a, wa)
    s2a, s2b = choose(o2a, e2a), None
    (e2b, o2b, xdb), (k, v), (c0, c1) = tick((e2b, o2b, xdb), (k, v), (c0, c1))
    e3b = E(o2b)
    o1v = O(v)
    xk0 = X(k)
    s2b = choose(o2b, e2b)
    wb = jnp.concatenate([db, xdb], axis=1)
    c0 = c0 + dot(hb, wb)
    c1 = c1 + dot(e1b, wb)
    r1 = seq_core(c1)
    r0 = seq_core(c0)
    (e3a,), (k, v), r1 = tick((e3a,), (k, v), r1)
    e1k = E(k)
    xv0 = X(v)
    c2 = dot(s2a, wa) + dot(s2b, wb)
    r2 = seq_core(c2)
    t1 = seq_y(*r1)
    (e3b, o1k, o1v), (v,), r2, t1 = tick((e3b, o1k, o1v), (v,), r2, t1)
    e1v = E(v)
    c3 = dot(choose(o1a, e3a), wa) + dot(choose(o1b, e3b), wb)
    r3 = seq_core(c3)
    q1 = z.swap(sum(t1), 1)
    t2 = seq_y(*r2)
    (e1k, xk0), r3, t2 = tick((e1k, xk0), r3, t2)
    e2k, o2k = E(o1k), O(e1k)
    xk1 = X(e1k)
    t3 = seq_y(*r3)
    q2 = z.swap(sum(t2), 2)
    (e1v, xv0, q1), t3, r0 = tick((e1v, xv0, q1), t3, r0)
    q3 = z.swap(sum(t3), 3)
    e2v, o2v = E(o1v), O(e1v)
    xv1 = X(e1v)
    t0 = seq_y(*r0)
    (e2k, o2k, xk1, q2), t0 = tick((e2k, o2k, xk1, q2), t0)
    e3k = E(o2k)
    k2 = choose(o2k, e2k)
    xk2 = X(k2)
    (e2v, o2v, xv1, q3), = tick((e2v, o2v, xv1, q3))
    e3v = E(o2v)
    v2 = choose(o2v, e2v)
    xv2 = X(v2)
    k3 = choose(o1k, e3k)
    v3 = choose(o1v, e3v)
    xk3, xv3 = X(k3), X(v3)
    kv_slots = [
        [[k, v], [xk0, xv0]],
        [[e1k, e1v], [xk1, xv1]],
        [[k2, v2], [xk2, xv2]],
        [[k3, v3], [xk3, xv3]],
    ]
    return kv_slots, [sum(t0), q1, q2, q3]


def on_device(
    mlp_hidden, encoder_stream, down_proj, final_gain, kv_proj, queries, out_proj, enc_len, dec_pad
):
    seq, dp = lax.axis_size("seq"), lax.axis_size("dp")
    nx = 1 << ((dp.bit_length() - 1) // 2)
    nz = dp // nx
    nc = 2
    ny = seq // nc
    z = Line("dp", dp, nz, nx)
    x = Line("dp", dp, nx, 1)
    y = Line("seq", seq, ny, nc)
    c = Line("seq", seq, nc, 1)

    hidden = mlp_hidden[0]
    enc_total, depth = hidden.shape
    rows = enc_total // seq
    block = down_proj.shape[1]
    width = block * dp
    dot = lambda a, b: jnp.dot(a, b, preferred_element_type=jnp.float32)

    half = depth // 2
    halves = [hidden[:, :half], hidden[:, half:]]
    downs = [down_proj[:half], down_proj[half:]]
    kv_local = [kv_proj[:, 0], kv_proj[:, 1]]

    def seq_core(part):
        part = part.reshape(ny, nc, rows, nx * block)
        pick = lambda i: lax.dynamic_index_in_dim(part, i, 1, keepdims=False)
        return pick(c.at), c.swap(pick(1 - c.at), 1)

    def seq_y(mine, theirs):
        part = mine + theirs
        total = lax.dynamic_index_in_dim(part, y.at, 0, keepdims=False)
        others = [
            y.swap(lax.dynamic_index_in_dim(part, y.at ^ k, 0, keepdims=False), k)
            for k in range(1, ny)
        ]
        return [total] + others

    def seq_sum(part):
        return sum(seq_y(*seq_core(part))[0:])

    if (nz, nx) == (4, 2):
        kv_slots, summed = woven(z, x, halves, downs, kv_local, dot, seq_core, seq_y)
    else:
        hidden_slots = z.gather(halves)
        down_slots = x.gather(downs)
        kv_slots = [x.gather(slot) for slot in z.gather(kv_local)]
        weights = [jnp.concatenate([s[p] for s in down_slots], axis=1) for p in range(2)]
        summed = []
        for m in range(nz):
            part = dot(hidden_slots[m][0], weights[0]) + dot(hidden_slots[m][1], weights[1])
            total = seq_sum(part)
            summed.append(total if m == 0 else z.swap(total, m))

    stream = encoder_stream[0]
    gain = final_gain.astype(jnp.float32)
    resid, gains = [], []
    for m in range(nz):
        for k in range(nx):
            start = ((z.at ^ m) * nx + (x.at ^ k)) * block
            piece = lax.dynamic_slice_in_dim(stream, start, block, 1).astype(jnp.float32)
            resid.append(piece + summed[m][:, k * block : (k + 1) * block])
            gains.append(lax.dynamic_slice_in_dim(gain, start, block, 0))
    resid = jnp.concatenate(resid, axis=1)
    gains = jnp.concatenate(gains, axis=0)
    spread = jnp.sum(resid * resid, axis=-1, keepdims=True) / width
    normed = (resid * lax.rsqrt(spread + 1e-06) * gains).astype(jnp.bfloat16)
    encoded, places = [], []
    for k, (far,) in enumerate(y.gather([normed])):
        encoded += [far, c.swap(far, 1)]
        for j in range(nc):
            start = ((y.at ^ k) * nc + (c.at ^ j)) * rows
            places.append(start + jnp.arange(rows, dtype=jnp.int32))
    encoded = jnp.concatenate(encoded, axis=0)
    visible = jnp.concatenate(places) < enc_len[0]

    keys = values = None
    for m in range(nz):
        for k in range(nx):
            at = (m * nx + k) * block
            piece = encoded[:, at : at + block]
            wk, wv = kv_slots[m][k]
            dk, dv = dot(piece, wk), dot(piece, wv)
            keys = dk if keys is None else keys + dk
            values = dv if values is None else values + dv
    keys = keys.astype(jnp.bfloat16)
    values = values.astype(jnp.bfloat16)

    heads_here = queries.shape[2] // HD
    dec_rows = queries.shape[1]
    attended = []
    for h in range(heads_here):
        cols = slice(h * HD, (h + 1) * HD)
        scores = lax.dot_general(
            queries[0][:, cols], keys[:, cols], (((1,), (1,)), ((), ())),
            preferred_element_type=jnp.float32,
        ) / math.sqrt(HD)
        scores = jnp.where(visible[None, :], scores, -jnp.inf)
        expo = jnp.exp(scores - jnp.max(scores, axis=-1, keepdims=True))
        attention = (expo / jnp.sum(expo, axis=-1, keepdims=True)).astype(jnp.bfloat16)
        attended.append(dot(attention, values[:, cols]).astype(jnp.bfloat16))
    attended = jnp.concatenate(attended, axis=1)
    row_live = jnp.arange(dec_rows, dtype=jnp.int32) < dec_rows - dec_pad[0]
    attended = jnp.where(row_live[:, None], attended, jnp.zeros_like(attended))

    out_rows = dec_rows // seq
    att = attended.reshape(ny, nc, out_rows, heads_here * HD)
    pick = lambda i: lax.dynamic_index_in_dim(att, i, 1, keepdims=False).reshape(
        ny * out_rows, heads_here * HD
    )
    part = dot(pick(c.at), out_proj) + c.swap(dot(pick(1 - c.at), out_proj), 1)
    part = part.reshape(ny, out_rows, width)
    total = lax.dynamic_index_in_dim(part, y.at, 0, keepdims=False)
    for k in range(1, ny):
        total = total + y.swap(lax.dynamic_index_in_dim(part, y.at ^ k, 0, keepdims=False), k)
    return total.astype(jnp.bfloat16)[None]


def solution(mesh):
    placed = (
        P("dp", None, "seq"),
        P("dp", "seq", None),
        P("seq", "dp"),
        P(),
        P("dp", None, "seq"),
        P("dp", None, "seq"),
        P("seq", None),
        P("dp"),
        P("dp"),
    )
    return jax.shard_map(
        on_device, mesh=mesh, in_specs=placed, out_specs=P("dp", "seq", None), check_vma=False
    )
```

```python
import math

import jax
import jax.numpy as jnp
from jax import lax
from jax.experimental import pallas as pl
from jax.experimental.pallas import tpu as pltpu
from jax.sharding import PartitionSpec as P

HD = 256
TILE = 256
F32, BF16 = jnp.float32, jnp.bfloat16
CHEAP = pl.CostEstimate(flops=1, bytes_accessed=1, transcendentals=0)
SOME = pl.CostEstimate(flops=1, bytes_accessed=1_800_000, transcendentals=0)


class Line:
    def __init__(self, name, total, size, stride):
        self.name, self.total, self.size, self.stride = name, total, size, stride
        self.at = (lax.axis_index(name) // stride) % size

    def place(self, index):
        return (index // self.stride) % self.size

    def shift(self, value, step):
        pairs = [
            (i, i + step * self.stride)
            for i in range(self.total)
            if 0 <= self.place(i) + step < self.size
        ]
        return lax.ppermute(value, self.name, pairs)

    def swap(self, value, mask):
        pairs = [
            (i, i + ((self.place(i) ^ mask) - self.place(i)) * self.stride)
            for i in range(self.total)
        ]
        return lax.ppermute(value, self.name, pairs)

    def cross(self, value):
        return self.turn(value, (0, 2, 1, 3))

    def ends(self, value):
        return self.turn(value, (3, 1, 2, 0))

    def turn(self, value, order):
        pairs = [
            (i, i + (order[self.place(i)] - self.place(i)) * self.stride) for i in range(self.total)
        ]
        return lax.ppermute(value, self.name, pairs)

    def gather(self, pieces):
        return [pieces] + [[self.swap(p, m) for p in pieces] for m in range(1, self.size)]


def tick(*groups):
    sizes = [len(g) for g in groups]
    flat = lax.optimization_barrier(tuple(v for g in groups for v in g))
    out, at = [], 0
    for size in sizes:
        out.append(list(flat[at : at + size]))
        at += size
    return out


def local(body, outs, *operands, scratch=(), cost=CHEAP, left=0):
    vmem = pl.BlockSpec(memory_space=pltpu.VMEM)
    stay = pl.BlockSpec(memory_space=pltpu.HBM)
    return pl.pallas_call(
        body,
        out_shape=[jax.ShapeDtypeStruct(shape, kind) for shape, kind in outs],
        in_specs=[pl.BlockSpec(memory_space=pltpu.SMEM)] + [stay] * left
        + [vmem] * (len(operands) - 1 - left),
        out_specs=[vmem] * len(outs),
        scratch_shapes=list(scratch),
        cost_estimate=cost,
        compiler_params=pltpu.CompilerParams(vmem_limit_bytes=12 << 20),
    )(*operands)


def mlp_part(at, pieces, downs, shape, first=0, sofar=None):
    ny, nc, rows = shape
    ways, halves = len(pieces[0]), len(pieces)
    flat = [p for half in pieces for p in half]
    total = ny * nc * rows
    depth = pieces[0][0].shape[1]
    block = downs[0].shape[1]
    before = list(sofar or ())

    def body(at_ref, *refs):
        lhs, refs = refs[: ways * halves], refs[ways * halves :]
        d0, d1 = refs[:2]
        adds, (mine, theirs, taken, sems) = refs[2:-4], refs[-4:]
        inner = (at_ref[0] == 1) | (at_ref[0] == 2)

        def fetch(h, way):
            cols = pl.ds(h * depth, depth)
            return pltpu.make_async_copy(lhs[ways * h + way], taken.at[:, cols], sems.at[h])

        for h in range(halves):
            if ways == 1:
                fetch(h, 0).start()
                continue

            @pl.when(inner)
            def _():
                fetch(h, 0).start()

            @pl.when(jnp.logical_not(inner))
            def _():
                fetch(h, 1).start()

        for h in range(halves):
            fetch(h, 0).wait()

        here = at_ref[3] == 0
        deep = slice(first * depth, (first + halves) * depth)
        for j, down in enumerate((d0, d1)):

            @pl.loop(0, block // TILE)
            def _(t):
                part = jnp.dot(
                    taken[...],
                    down[deep, pl.ds(pl.multiple_of(t * TILE, TILE), TILE)],
                    preferred_element_type=F32,
                )
                cols = pl.ds(pl.multiple_of(j * block + t * TILE, TILE), TILE)
                for i in range(ny):
                    to = slice(i * rows, (i + 1) * rows)
                    one = part[(2 * i) * rows : (2 * i + 1) * rows]
                    two = part[(2 * i + 1) * rows : (2 * i + 2) * rows]
                    own, far = jnp.where(here, one, two), jnp.where(here, two, one)
                    if adds:
                        own, far = own + adds[0][to, cols], far + adds[1][to, cols]
                    mine[to, cols] = own
                    theirs[to, cols] = far

    out = ((ny * rows, 2 * block), F32)
    return local(
        body, [out, out], at, *flat, *downs, *before,
        scratch=[pltpu.VMEM((total, halves * depth), BF16), pltpu.SemaphoreType.DMA((halves,))],
        cost=SOME, left=len(flat),
    )


def core_add(at, mine, theirs):
    rows, cols = mine.shape[0] // 2, mine.shape[1]

    def body(at_ref, mine_ref, theirs_ref, keep, send):
        first = at_ref[2] == 0
        one = mine_ref[:rows] + theirs_ref[:rows]
        two = mine_ref[rows:] + theirs_ref[rows:]
        keep[...] = jnp.where(first, one, two)
        send[...] = jnp.where(first, two, one)

    return local(body, [((rows, cols), F32)] * 2, at, mine, theirs)


def norm_part(at, keep, came, others, stream, gain):
    rows, cols = keep.shape
    block = cols // 2

    def body(at_ref, keep_ref, came_ref, q10, q11, q2, q3, stream_ref, gain_ref, near, far, resid):
        zat, xat = at_ref[0], at_ref[1]
        square = jnp.zeros((rows, 1), F32)
        starts = []
        for m, ref in enumerate((None, (q10, q11), q2, q3)):
            for k in range(2):
                start = pl.multiple_of(((zat ^ m) * 2 + (xat ^ k)) * block, block)
                starts.append(start)
                here = slice(k * block, (k + 1) * block)
                if m == 0:
                    add = keep_ref[:, here] + came_ref[:, here]
                else:
                    add = ref[k][...] if m == 1 else ref[:, here]
                value = stream_ref[:, pl.ds(start, block)].astype(F32) + add
                square = square + jnp.sum(value * value, axis=-1, keepdims=True)
                at = (2 * m + k) * block
                resid[:, at : at + block] = value
        scale = lax.rsqrt(square / (8 * block) + 1e-06)
        for m, (ref, half) in enumerate(((near, 0), (far, 0), (far, 1), (near, 1))):
            for k in range(2):
                at = (2 * m + k) * block
                row = gain_ref[:, pl.ds(starts[2 * m + k], block)].astype(F32)
                to = (2 * half + k) * block
                ref[:, to : to + block] = (resid[:, at : at + block] * scale * row).astype(BF16)

    out = ((rows, 4 * block), BF16)
    return local(
        body, [out, out], at, keep, came, *others, stream, gain,
        scratch=[pltpu.VMEM((rows, 8 * block), F32)],
    )


def kv_part(at, rows, weights):
    count, width = rows.shape
    depth, cols = weights[0].shape

    def body(at_ref, *refs):
        (lhs, out, held, sems) = refs[4:]
        loads = [pltpu.make_async_copy(refs[p], held.at[p], sems.at[p]) for p in range(4)]
        for load in loads:
            load.start()
        for p, load in enumerate(loads):
            load.wait()
            for t in range(cols // TILE):
                here = slice(t * TILE, (t + 1) * TILE)
                part = jnp.dot(
                    lhs[:, p * depth : (p + 1) * depth],
                    held[p, :, here],
                    preferred_element_type=F32,
                )
                out[:, here] = part if p == 0 else out[:, here] + part

    return local(
        body, [((count, cols), F32)], at, *weights, rows,
        scratch=[pltpu.VMEM((4, depth, cols), BF16), pltpu.SemaphoreType.DMA((4,))],
        left=4,
    )[0]


def woven(z, x, y, c, hidden, down, kv, stream, gain, rows):
    E, O, X, Y = (lambda v: z.swap(v, 1)), z.cross, (lambda v: x.swap(v, 1)), (lambda v: y.swap(v, 1))
    C = lambda v: c.swap(v, 1)
    at = jnp.stack([z.at, x.at, y.at, c.at]).astype(jnp.int32)
    inner = (z.at == 1) | (z.at == 2)
    half = hidden.shape[1] // 2
    ha, hb = hidden[:, :half], hidden[:, half:]
    k, v = kv
    product = lambda pieces, xd, **more: mlp_part(at, pieces, (down, xd), (2, 2, rows), **more)

    e1a, o1a, xd = E(ha), O(ha), X(down)
    e1b, o1b = E(hb), O(hb)
    e2a, o2a = E(o1a), O(e1a)
    e2b, o2b = E(o1b), O(e1b)
    e3a, e3b = E(o2a), E(o2b)

    (o2a,), (k, v) = tick((o2a,), (k, v))
    ok, ov, xk0 = O(k), O(v), X(k)
    (e2a, o2a, e2b, o2b, xd), (k, v) = tick((e2a, o2a, e2b, o2b, xd), (k, v))
    m1, h1 = product(((e1a,), (e1b,)), xd)
    m2, h2 = product(((o2a, e2a), (o2b, e2b)), xd)
    m0, h0 = product(((ha,), (hb,)), xd)
    part3 = product(((o1a, e3a),), xd)

    done = (m1, h1, m2, h2, m0, h0, e3b, ok, ov, xk0, *part3)
    (m1, h1, m2, h2, m0, h0, e3b, ok, ov, xk0, *part3), (k, v) = tick(done, (k, v))
    fk, fv = z.ends(k), z.ends(v)
    xv0 = X(v)
    h1, h2, h0 = C(h1), C(h2), C(h0)
    m3, h3 = product(((o1b, e3b),), xd, first=1, sofar=part3)

    (h1, h2, h0, m3, h3), = tick((h1, h2, h0, m3, h3))
    h3 = C(h3)
    k2, s2 = core_add(at, m2, h2)
    s2 = Y(s2)
    k1, s1 = core_add(at, m1, h1)
    k0, s0 = core_add(at, m0, h0)

    (h3, k1, s1, k0, s0), = tick((h3, k1, s1, k0, s0))
    k3, s3 = core_add(at, m3, h3)
    s3 = Y(s3)

    (s2,), (s1, s0) = tick((s2,), (s1, s0))
    q2 = z.swap(k2 + s2, 2)
    s1 = Y(s1)

    (s3, fk, xv0), (s0,) = tick((s3, fk, xv0), (s0,))
    q3 = z.swap(k3 + s3, 3)
    s0 = Y(s0)
    kk = jnp.where(inner, ok, fk)
    xkk = X(kk)

    (s1, fv), = tick((s1, fv))
    q1 = k1 + s1
    q1 = [z.swap(part, 1) for part in jnp.split(q1, 2, axis=1)]
    vv = jnp.where(inner, ov, fv)

    (q2, q3, s0, xkk), q1, (vv,) = tick((q2, q3, s0, xkk), q1, (vv,))
    xvv = X(vv)
    mine, other = norm_part(at, k0, s0, (*q1, q2, q3), stream, gain)
    near, far = E(other), Y(mine)
    (near, far), = tick((near, far))
    nearfar = Y(near)
    near2, mine2, far2 = C(near), C(mine), C(far)
    (nearfar, near2, mine2, far2), = tick((nearfar, near2, mine2, far2))
    pair = jnp.concatenate([near, near2, nearfar, C(nearfar)], axis=0)
    own = [jnp.concatenate([mine, mine2, far, far2], axis=0)]
    wk, wv = (k, xk0, kk, xkk), (v, xv0, vv, xvv)
    keys = E(kv_part(at, pair, wk))
    values = kv_part(at, pair, wv)
    (values,), (own,) = tick((values,), own)
    values = E(values)
    return kv_part(at, own, wk) + keys, kv_part(at, own, wv) + values


def on_device(
    mlp_hidden, encoder_stream, down_proj, final_gain, kv_proj, queries, out_proj, enc_len, dec_pad
):
    seq, dp = lax.axis_size("seq"), lax.axis_size("dp")
    nx = 1 << ((dp.bit_length() - 1) // 2)
    nz = dp // nx
    nc = 2
    ny = seq // nc
    z = Line("dp", dp, nz, nx)
    x = Line("dp", dp, nx, 1)
    y = Line("seq", seq, ny, nc)
    c = Line("seq", seq, nc, 1)

    hidden = mlp_hidden[0]
    enc_total, depth = hidden.shape
    rows = enc_total // seq
    block = down_proj.shape[1]
    width = block * dp
    dot = lambda a, b: jnp.dot(a, b, preferred_element_type=jnp.float32)

    half = depth // 2
    halves = [hidden[:, :half], hidden[:, half:]]
    downs = [down_proj[:half], down_proj[half:]]
    kv_local = [kv_proj[:, 0], kv_proj[:, 1]]

    def seq_core(part):
        part = part.reshape(ny, nc, rows, nx * block)
        pick = lambda i: lax.dynamic_index_in_dim(part, i, 1, keepdims=False)
        return pick(c.at), c.swap(pick(1 - c.at), 1)

    def seq_y(mine, theirs):
        part = mine + theirs
        total = lax.dynamic_index_in_dim(part, y.at, 0, keepdims=False)
        others = [
            y.swap(lax.dynamic_index_in_dim(part, y.at ^ k, 0, keepdims=False), k)
            for k in range(1, ny)
        ]
        return [total] + others

    stream = encoder_stream[0]
    gain = final_gain.astype(jnp.float32)

    def norm(summed):
        resid, gains = [], []
        for m in range(nz):
            for k in range(nx):
                start = ((z.at ^ m) * nx + (x.at ^ k)) * block
                piece = lax.dynamic_slice_in_dim(stream, start, block, 1).astype(jnp.float32)
                resid.append(piece + summed[m][:, k * block : (k + 1) * block])
                gains.append(lax.dynamic_slice_in_dim(gain, start, block, 0))
        resid = jnp.concatenate(resid, axis=1)
        gains = jnp.concatenate(gains, axis=0)
        spread = jnp.sum(resid * resid, axis=-1, keepdims=True) / width
        return (resid * lax.rsqrt(spread + 1e-06) * gains).astype(jnp.bfloat16)

    places = []
    for k in range(ny):
        for j in range(nc):
            start = ((y.at ^ k) * nc + (c.at ^ j)) * rows
            places.append(start + jnp.arange(rows, dtype=jnp.int32))
    visible = jnp.concatenate(places) < enc_len[0]

    if (nz, nx, ny) == (4, 2, 2):
        keys, values = woven(
            z, x, y, c, hidden, down_proj, kv_local, stream, final_gain[None], rows
        )
    else:
        hidden_slots = z.gather(halves)
        down_slots = x.gather(downs)
        kv_slots = [x.gather(slot) for slot in z.gather(kv_local)]
        weights = [jnp.concatenate([s[p] for s in down_slots], axis=1) for p in range(2)]
        summed = []
        for m in range(nz):
            part = dot(hidden_slots[m][0], weights[0]) + dot(hidden_slots[m][1], weights[1])
            total = sum(seq_y(*seq_core(part)))
            summed.append(total if m == 0 else z.swap(total, m))
        encoded = []
        for (far,) in y.gather([norm(summed)]):
            encoded += [far, c.swap(far, 1)]
        encoded = jnp.concatenate(encoded, axis=0)
        keys = values = 0.0
        for m in range(nz):
            for k in range(nx):
                at = (m * nx + k) * block
                piece = encoded[:, at : at + block]
                keys = keys + dot(piece, kv_slots[m][k][0])
                values = values + dot(piece, kv_slots[m][k][1])
    keys = keys.astype(jnp.bfloat16)
    values = values.astype(jnp.bfloat16)

    heads_here = queries.shape[2] // HD
    dec_rows = queries.shape[1]
    attended = []
    for h in range(heads_here):
        cols = slice(h * HD, (h + 1) * HD)
        scores = lax.dot_general(
            queries[0][:, cols], keys[:, cols], (((1,), (1,)), ((), ())),
            preferred_element_type=jnp.float32,
        ) / math.sqrt(HD)
        scores = jnp.where(visible[None, :], scores, -jnp.inf)
        expo = jnp.exp(scores - jnp.max(scores, axis=-1, keepdims=True))
        attention = (expo / jnp.sum(expo, axis=-1, keepdims=True)).astype(jnp.bfloat16)
        attended.append(dot(attention, values[:, cols]).astype(jnp.bfloat16))
    attended = jnp.concatenate(attended, axis=1)
    row_live = jnp.arange(dec_rows, dtype=jnp.int32) < dec_rows - dec_pad[0]
    attended = jnp.where(row_live[:, None], attended, jnp.zeros_like(attended))

    out_rows = dec_rows // seq
    att = attended.reshape(ny, nc, out_rows, heads_here * HD)
    pick = lambda i: lax.dynamic_index_in_dim(att, i, 1, keepdims=False).reshape(
        ny * out_rows, heads_here * HD
    )
    part = dot(pick(c.at), out_proj) + c.swap(dot(pick(1 - c.at), out_proj), 1)
    part = part.reshape(ny, out_rows, width)
    total = lax.dynamic_index_in_dim(part, y.at, 0, keepdims=False)
    for k in range(1, ny):
        other = lax.dynamic_index_in_dim(part, y.at ^ k, 0, keepdims=False).astype(BF16)
        total = total + y.swap(other, k).astype(F32)
    return total.astype(jnp.bfloat16)[None]


def solution(mesh):
    placed = (
        P("dp", None, "seq"),
        P("dp", "seq", None),
        P("seq", "dp"),
        P(),
        P("dp", None, "seq"),
        P("dp", None, "seq"),
        P("seq", None),
        P("dp"),
        P("dp"),
    )
    return jax.shard_map(
        on_device, mesh=mesh, in_specs=placed, out_specs=P("dp", "seq", None), check_vma=False
    )
```

```python
import math

import jax
import jax.numpy as jnp
from jax import lax
from jax.experimental import pallas as pl
from jax.experimental.pallas import tpu as pltpu
from jax.sharding import PartitionSpec as P

HD = 256
TILE = 256
F32, BF16 = jnp.float32, jnp.bfloat16


def cost(us):
    return pl.CostEstimate(flops=1, bytes_accessed=int(1 + us * 3_500_000), transcendentals=0)


CHEAP, SOME = cost(0), cost(0.5)


class Line:
    def __init__(self, name, total, size, stride):
        self.name, self.total, self.size, self.stride = name, total, size, stride
        self.at = (lax.axis_index(name) // stride) % size

    def place(self, index):
        return (index // self.stride) % self.size

    def shift(self, value, step):
        pairs = [
            (i, i + step * self.stride)
            for i in range(self.total)
            if 0 <= self.place(i) + step < self.size
        ]
        return lax.ppermute(value, self.name, pairs)

    def swap(self, value, mask):
        pairs = [
            (i, i + ((self.place(i) ^ mask) - self.place(i)) * self.stride)
            for i in range(self.total)
        ]
        return lax.ppermute(value, self.name, pairs)

    def cross(self, value):
        return self.turn(value, (0, 2, 1, 3))

    def ends(self, value):
        return self.turn(value, (3, 1, 2, 0))

    def turn(self, value, order):
        pairs = [
            (i, i + (order[self.place(i)] - self.place(i)) * self.stride) for i in range(self.total)
        ]
        return lax.ppermute(value, self.name, pairs)

    def gather(self, pieces):
        return [pieces] + [[self.swap(p, m) for p in pieces] for m in range(1, self.size)]


def tick(*groups):
    sizes = [len(g) for g in groups]
    flat = lax.optimization_barrier(tuple(v for g in groups for v in g))
    out, at = [], 0
    for size in sizes:
        out.append(list(flat[at : at + size]))
        at += size
    return out


def local(body, outs, *operands, scratch=(), paced=CHEAP, left=0):
    vmem = pl.BlockSpec(memory_space=pltpu.VMEM)
    stay = pl.BlockSpec(memory_space=pltpu.HBM)
    return pl.pallas_call(
        body,
        out_shape=[jax.ShapeDtypeStruct(shape, kind) for shape, kind in outs],
        in_specs=[pl.BlockSpec(memory_space=pltpu.SMEM)] + [stay] * left
        + [vmem] * (len(operands) - 1 - left),
        out_specs=[vmem] * len(outs),
        scratch_shapes=list(scratch),
        cost_estimate=paced,
        compiler_params=pltpu.CompilerParams(vmem_limit_bytes=12 << 20),
    )(*operands)


def mlp_part(at, pieces, downs, shape, first=0, sofar=None):
    ny, nc, rows = shape
    ways, halves = len(pieces[0]), len(pieces)
    flat = [p for half in pieces for p in half]
    total = ny * nc * rows
    depth = pieces[0][0].shape[1]
    block = downs[0].shape[1]
    before = list(sofar or ())

    def body(at_ref, *refs):
        lhs, refs = refs[: ways * halves], refs[ways * halves :]
        d0, d1 = refs[:2]
        adds, (mine, theirs, taken, sems) = refs[2:-4], refs[-4:]
        inner = (at_ref[0] == 1) | (at_ref[0] == 2)

        def fetch(h, way):
            cols = pl.ds(h * depth, depth)
            return pltpu.make_async_copy(lhs[ways * h + way], taken.at[:, cols], sems.at[h])

        for h in range(halves):
            if ways == 1:
                fetch(h, 0).start()
                continue

            @pl.when(inner)
            def _():
                fetch(h, 0).start()

            @pl.when(jnp.logical_not(inner))
            def _():
                fetch(h, 1).start()

        for h in range(halves):
            fetch(h, 0).wait()

        here = at_ref[3] == 0
        deep = slice(first * depth, (first + halves) * depth)
        for j, down in enumerate((d0, d1)):

            @pl.loop(0, block // TILE)
            def _(t):
                part = jnp.dot(
                    taken[...],
                    down[deep, pl.ds(pl.multiple_of(t * TILE, TILE), TILE)],
                    preferred_element_type=F32,
                )
                cols = pl.ds(pl.multiple_of(j * block + t * TILE, TILE), TILE)
                for i in range(ny):
                    to = slice(i * rows, (i + 1) * rows)
                    one = part[(2 * i) * rows : (2 * i + 1) * rows]
                    two = part[(2 * i + 1) * rows : (2 * i + 2) * rows]
                    own, far = jnp.where(here, one, two), jnp.where(here, two, one)
                    if adds:
                        own, far = own + adds[0][to, cols], far + adds[1][to, cols]
                    mine[to, cols] = own
                    theirs[to, cols] = far

    out = ((ny * rows, 2 * block), F32)
    return local(
        body, [out, out], at, *flat, *downs, *before,
        scratch=[pltpu.VMEM((total, halves * depth), BF16), pltpu.SemaphoreType.DMA((halves,))],
        paced=SOME, left=len(flat),
    )


def core_add(at, mine, theirs, sent=F32):
    rows, cols = mine.shape[0] // 2, mine.shape[1]

    def body(at_ref, mine_ref, theirs_ref, keep, send):
        first = at_ref[2] == 0
        one = mine_ref[:rows] + theirs_ref[:rows]
        two = mine_ref[rows:] + theirs_ref[rows:]
        keep[...] = jnp.where(first, one, two)
        send[...] = jnp.where(first, two, one).astype(sent)

    return local(body, [((rows, cols), F32), ((rows, cols), sent)], at, mine, theirs)


def norm_part(at, keep, came, others, stream, gain):
    rows, cols = keep.shape
    block = cols // 2

    def body(at_ref, keep_ref, came_ref, q1, q2, q3, stream_ref, gain_ref, near, far, resid):
        zat, xat = at_ref[0], at_ref[1]
        square = jnp.zeros((rows, 1), F32)
        starts = []
        for m, ref in enumerate((None, q1, q2, q3)):
            for k in range(2):
                start = pl.multiple_of(((zat ^ m) * 2 + (xat ^ k)) * block, block)
                starts.append(start)
                here = slice(k * block, (k + 1) * block)
                if m == 0:
                    add = keep_ref[:, here] + came_ref[:, here]
                else:
                    add = ref[:, here]
                value = stream_ref[:, pl.ds(start, block)].astype(F32) + add
                square = square + jnp.sum(value * value, axis=-1, keepdims=True)
                at = (2 * m + k) * block
                resid[:, at : at + block] = value
        scale = lax.rsqrt(square / (8 * block) + 1e-06)
        for m, (ref, half) in enumerate(((near, 0), (far, 0), (far, 1), (near, 1))):
            for k in range(2):
                at = (2 * m + k) * block
                row = gain_ref[:, pl.ds(starts[2 * m + k], block)].astype(F32)
                to = (2 * half + k) * block
                ref[:, to : to + block] = (resid[:, at : at + block] * scale * row).astype(BF16)

    out = ((rows, 4 * block), BF16)
    return local(
        body, [out, out], at, keep, came, *others, stream, gain,
        scratch=[pltpu.VMEM((rows, 8 * block), F32)],
    )


def kv_part(at, rows, wk, wv, paced=CHEAP):
    count, width = rows[0].shape
    depth, cols = wk[0].shape
    pieces, parts = len(rows), len(wk) + len(wv)
    weights = [*wk, *wv]
    total = pieces * count

    def body(at_ref, *refs):
        out, stack, held, sems = refs[parts + pieces :]
        copies = [
            pltpu.make_async_copy(
                refs[parts + i], stack.at[pl.ds(i * count, count)], sems.at[parts + i]
            )
            for i in range(pieces)
        ]
        loads = [pltpu.make_async_copy(refs[p], held.at[p], sems.at[p]) for p in range(parts)]
        for copy in copies + loads:
            copy.start()
        for copy in copies:
            copy.wait()
        for p, load in enumerate(loads):
            load.wait()
            m = p % len(wk)
            to = slice(0, total) if p < len(wk) else slice(total, 2 * total)
            for t in range(cols // TILE):
                here = slice(t * TILE, (t + 1) * TILE)
                part = jnp.dot(
                    stack[:, m * depth : (m + 1) * depth],
                    held[p, :, here],
                    preferred_element_type=F32,
                )
                out[to, here] = part if m == 0 else out[to, here] + part

    return local(
        body, [((2 * total, cols), F32)], at, *weights, *rows,
        scratch=[
            pltpu.VMEM((total, width), BF16),
            pltpu.VMEM((parts, depth, cols), BF16),
            pltpu.SemaphoreType.DMA((parts + pieces,)),
        ],
        left=parts + pieces, paced=paced,
    )[0]


def softmax_part(at, own, came, queries, visible):
    total, cols = own.shape[0] // 2, own.shape[1]
    half = total // 2
    dec = queries.shape[0]
    heads = cols // HD

    def body(at_ref, own_ref, one, two, query, seen, out, keys):
        keys[:half] = (own_ref[:half] + one[:half]).astype(BF16)
        keys[half:] = (own_ref[half:total] + two[:half]).astype(BF16)
        for h in range(heads):
            here = slice(h * HD, (h + 1) * HD)
            scores = lax.dot_general(
                query[:, here], keys[:, here], (((1,), (1,)), ((), ())),
                preferred_element_type=F32,
            ) / math.sqrt(HD)
            scores = jnp.where(seen[...] > 0, scores, -jnp.inf)
            expo = jnp.exp(scores - jnp.max(scores, axis=-1, keepdims=True))
            weight = expo / jnp.sum(expo, axis=-1, keepdims=True)
            out[h * dec : (h + 1) * dec] = weight.astype(BF16)

    return local(
        body, [((heads * dec, total), BF16)], at, own, *came, queries, visible,
        scratch=[pltpu.VMEM((total, cols), BF16)], paced=CHEAP,
    )[0]


def out_part(at, own, came, weights, out_proj):
    total, cols = own.shape[0] // 2, own.shape[1]
    half = total // 2
    heads = cols // HD
    dec = weights.shape[0] // heads
    rows = dec // 4
    width = out_proj.shape[1]
    wide = 512

    def body(at_ref, own_ref, one, two, weight, proj, mine, theirs, values, attended, order):
        values[:half] = (own_ref[total : total + half] + one[half:]).astype(BF16)
        values[half:] = (own_ref[total + half :] + two[half:]).astype(BF16)
        live = lax.broadcasted_iota(jnp.int32, (dec, HD), 0) < dec - at_ref[5]
        for h in range(heads):
            here = slice(h * HD, (h + 1) * HD)
            value = jnp.dot(
                weight[h * dec : (h + 1) * dec], values[:, here], preferred_element_type=F32
            )
            attended[:, here] = jnp.where(live, value, 0.0).astype(BF16)
        first = at_ref[3] == 0
        for i in range(2):
            a = attended[(2 * i) * rows : (2 * i + 1) * rows]
            b = attended[(2 * i + 1) * rows : (2 * i + 2) * rows]
            order[i * rows : (i + 1) * rows] = jnp.where(first, a, b)
            order[(2 + i) * rows : (3 + i) * rows] = jnp.where(first, b, a)

        for t in range(width // wide):
            here = slice(t * wide, (t + 1) * wide)
            part = jnp.dot(order[...], proj[:, here], preferred_element_type=F32)
            mine[:, here] = part[: 2 * rows]
            theirs[:, here] = part[2 * rows :]

    return local(
        body, [((2 * rows, width), F32)] * 2, at, own, *came, weights, out_proj,
        scratch=[
            pltpu.VMEM((total, cols), BF16),
            pltpu.VMEM((dec, cols), BF16),
            pltpu.VMEM((dec, cols), BF16),
        ],
    )


def woven(z, x, y, c, hidden, down, kv, stream, gain, rows, query, out_proj, visible, pad):
    E, O, X, Y = (lambda v: z.swap(v, 1)), z.cross, (lambda v: x.swap(v, 1)), (lambda v: y.swap(v, 1))
    C = lambda v: c.swap(v, 1)
    at = jnp.stack([z.at, x.at, y.at, c.at, z.at, pad]).astype(jnp.int32)
    inner = (z.at == 1) | (z.at == 2)
    half = hidden.shape[1] // 2
    ha, hb = hidden[:, :half], hidden[:, half:]
    k, v = kv
    product = lambda pieces, xd, **more: mlp_part(at, pieces, (down, xd), (2, 2, rows), **more)

    e1a, o1a, xd = E(ha), O(ha), X(down)
    e1b, o1b = E(hb), O(hb)
    e2a, o2a = E(o1a), O(e1a)
    e2b, o2b = E(o1b), O(e1b)
    e3a, e3b = E(o2a), E(o2b)

    (o2a,), (k, v) = tick((o2a,), (k, v))
    ok, ov, xk0 = O(k), O(v), X(k)
    (e2a, o2a, e2b, o2b, xd), (k, v) = tick((e2a, o2a, e2b, o2b, xd), (k, v))
    m1, h1 = product(((e1a,), (e1b,)), xd)
    m2, h2 = product(((o2a, e2a), (o2b, e2b)), xd)
    m0, h0 = product(((ha,), (hb,)), xd)
    part3 = product(((o1a, e3a),), xd)

    done = (m1, h1, m2, h2, m0, h0, e3b, ok, ov, xk0, *part3)
    (m1, h1, m2, h2, m0, h0, e3b, ok, ov, xk0, *part3), (k, v) = tick(done, (k, v))
    fk, fv = z.ends(k), z.ends(v)
    xv0 = X(v)
    h1, h2, h0 = C(h1), C(h2), C(h0)
    m3, h3 = product(((o1b, e3b),), xd, first=1, sofar=part3)

    (h1, h2, h0, m3, h3), = tick((h1, h2, h0, m3, h3))
    h3 = C(h3)
    k2, s2 = core_add(at, m2, h2)
    s2 = Y(s2)
    k1, s1 = core_add(at, m1, h1)
    k0, s0 = core_add(at, m0, h0)

    (h3, k1, s1, k0, s0), = tick((h3, k1, s1, k0, s0))
    k3, s3 = core_add(at, m3, h3)
    s3 = Y(s3)

    (s2,), (s1, s0) = tick((s2,), (s1, s0))
    q2 = z.swap(k2 + s2, 2)
    s1 = Y(s1)

    (s3, fk, xv0), (s0, v, ov) = tick((s3, fk, xv0), (s0, v, ov))
    q3 = z.swap(k3 + s3, 3)
    s0 = Y(s0)
    kk = jnp.where(inner, ok, fk)
    xkk = X(kk)

    (s1,), = tick((s1,))
    q1 = z.swap(k1 + s1, 1)

    vv = jnp.where(inner, ov, fv)
    xvv = X(vv)
    (q1, q2, q3, s0, xkk), = tick((q1, q2, q3, s0, xkk))
    mine, other = norm_part(at, k0, s0, (q1, q2, q3), stream, gain)
    near, far = E(other), Y(mine)
    (near, far, xvv), = tick((near, far, xvv))
    nearfar = Y(near)
    near2, mine2, far2 = C(near), C(mine), C(far)
    (near2,), = tick((near2,))
    wk, wv = (k, xk0, kk, xkk), (v, xv0, vv, xvv)
    sums1 = E(kv_part(at, (near, near2), wk, wv))
    nearfar2 = C(nearfar)
    sums2 = kv_part(at, (nearfar, nearfar2), wk, wv, cost(1))
    came = sums1, E(sums2)
    (sums2,), own = tick((sums2,), (mine, mine2, far, far2))
    sums = kv_part(at, own, wk, wv)
    weight = softmax_part(at, sums, came, query, visible)
    m, h = out_part(at, sums, came, weight, out_proj)
    keep, send = core_add(at, m, C(h), BF16)
    return (keep + Y(send).astype(F32)).astype(BF16)


def on_device(
    mlp_hidden, encoder_stream, down_proj, final_gain, kv_proj, queries, out_proj, enc_len, dec_pad
):
    seq, dp = lax.axis_size("seq"), lax.axis_size("dp")
    nx = 1 << ((dp.bit_length() - 1) // 2)
    nz = dp // nx
    nc = 2
    ny = seq // nc
    z = Line("dp", dp, nz, nx)
    x = Line("dp", dp, nx, 1)
    y = Line("seq", seq, ny, nc)
    c = Line("seq", seq, nc, 1)

    hidden = mlp_hidden[0]
    enc_total, depth = hidden.shape
    rows = enc_total // seq
    block = down_proj.shape[1]
    width = block * dp
    dot = lambda a, b: jnp.dot(a, b, preferred_element_type=jnp.float32)

    half = depth // 2
    halves = [hidden[:, :half], hidden[:, half:]]
    downs = [down_proj[:half], down_proj[half:]]
    kv_local = [kv_proj[:, 0], kv_proj[:, 1]]

    def seq_core(part):
        part = part.reshape(ny, nc, rows, nx * block)
        pick = lambda i: lax.dynamic_index_in_dim(part, i, 1, keepdims=False)
        return pick(c.at), c.swap(pick(1 - c.at), 1)

    def seq_y(mine, theirs):
        part = mine + theirs
        total = lax.dynamic_index_in_dim(part, y.at, 0, keepdims=False)
        others = [
            y.swap(lax.dynamic_index_in_dim(part, y.at ^ k, 0, keepdims=False), k)
            for k in range(1, ny)
        ]
        return [total] + others

    stream = encoder_stream[0]
    gain = final_gain.astype(jnp.float32)

    def norm(summed):
        resid, gains = [], []
        for m in range(nz):
            for k in range(nx):
                start = ((z.at ^ m) * nx + (x.at ^ k)) * block
                piece = lax.dynamic_slice_in_dim(stream, start, block, 1).astype(jnp.float32)
                resid.append(piece + summed[m][:, k * block : (k + 1) * block])
                gains.append(lax.dynamic_slice_in_dim(gain, start, block, 0))
        resid = jnp.concatenate(resid, axis=1)
        gains = jnp.concatenate(gains, axis=0)
        spread = jnp.sum(resid * resid, axis=-1, keepdims=True) / width
        return (resid * lax.rsqrt(spread + 1e-06) * gains).astype(jnp.bfloat16)

    places = []
    for k in range(ny):
        for j in range(nc):
            start = ((y.at ^ k) * nc + (c.at ^ j)) * rows
            places.append(start + jnp.arange(rows, dtype=jnp.int32))
    visible = jnp.concatenate(places) < enc_len[0]

    if (nz, nx, ny) == (4, 2, 2):
        return woven(
            z, x, y, c, hidden, down_proj, kv_local, stream, final_gain[None], rows, queries[0],
            out_proj, visible.astype(jnp.int32)[None], dec_pad[0],
        )[None]
    else:
        hidden_slots = z.gather(halves)
        down_slots = x.gather(downs)
        kv_slots = [x.gather(slot) for slot in z.gather(kv_local)]
        weights = [jnp.concatenate([s[p] for s in down_slots], axis=1) for p in range(2)]
        summed = []
        for m in range(nz):
            part = dot(hidden_slots[m][0], weights[0]) + dot(hidden_slots[m][1], weights[1])
            total = sum(seq_y(*seq_core(part)))
            summed.append(total if m == 0 else z.swap(total, m))
        encoded = []
        for (far,) in y.gather([norm(summed)]):
            encoded += [far, c.swap(far, 1)]
        encoded = jnp.concatenate(encoded, axis=0)
        keys = values = 0.0
        for m in range(nz):
            for k in range(nx):
                at = (m * nx + k) * block
                piece = encoded[:, at : at + block]
                keys = keys + dot(piece, kv_slots[m][k][0])
                values = values + dot(piece, kv_slots[m][k][1])
    keys = keys.astype(jnp.bfloat16)
    values = values.astype(jnp.bfloat16)

    heads_here = queries.shape[2] // HD
    dec_rows = queries.shape[1]
    attended = []
    for h in range(heads_here):
        cols = slice(h * HD, (h + 1) * HD)
        scores = lax.dot_general(
            queries[0][:, cols], keys[:, cols], (((1,), (1,)), ((), ())),
            preferred_element_type=jnp.float32,
        ) / math.sqrt(HD)
        scores = jnp.where(visible[None, :], scores, -jnp.inf)
        expo = jnp.exp(scores - jnp.max(scores, axis=-1, keepdims=True))
        attention = (expo / jnp.sum(expo, axis=-1, keepdims=True)).astype(jnp.bfloat16)
        attended.append(dot(attention, values[:, cols]).astype(jnp.bfloat16))
    attended = jnp.concatenate(attended, axis=1)
    row_live = jnp.arange(dec_rows, dtype=jnp.int32) < dec_rows - dec_pad[0]
    attended = jnp.where(row_live[:, None], attended, jnp.zeros_like(attended))

    out_rows = dec_rows // seq
    att = attended.reshape(ny, nc, out_rows, heads_here * HD)
    pick = lambda i: lax.dynamic_index_in_dim(att, i, 1, keepdims=False).reshape(
        ny * out_rows, heads_here * HD
    )
    part = dot(pick(c.at), out_proj) + c.swap(dot(pick(1 - c.at), out_proj), 1)
    part = part.reshape(ny, out_rows, width)
    total = lax.dynamic_index_in_dim(part, y.at, 0, keepdims=False)
    for k in range(1, ny):
        other = lax.dynamic_index_in_dim(part, y.at ^ k, 0, keepdims=False).astype(BF16)
        total = total + y.swap(other, k).astype(F32)
    return total.astype(jnp.bfloat16)[None]


def solution(mesh):
    placed = (
        P("dp", None, "seq"),
        P("dp", "seq", None),
        P("seq", "dp"),
        P(),
        P("dp", None, "seq"),
        P("dp", None, "seq"),
        P("seq", None),
        P("dp"),
        P("dp"),
    )
    return jax.shard_map(
        on_device, mesh=mesh, in_specs=placed, out_specs=P("dp", "seq", None), check_vma=False
    )
```

```python
import math

import jax
import jax.numpy as jnp
from jax import lax
from jax.experimental import pallas as pl
from jax.experimental.pallas import tpu as pltpu
from jax.sharding import PartitionSpec as P

HD = 256
TILE = 256
F32, BF16 = jnp.float32, jnp.bfloat16


def cost(us):
    return pl.CostEstimate(flops=1, bytes_accessed=int(1 + us * 3_500_000), transcendentals=0)


CHEAP, SOME = cost(0), cost(0.5)


class Line:
    def __init__(self, name, total, size, stride):
        self.name, self.total, self.size, self.stride = name, total, size, stride
        self.at = (lax.axis_index(name) // stride) % size

    def place(self, index):
        return (index // self.stride) % self.size

    def shift(self, value, step):
        pairs = [
            (i, i + step * self.stride)
            for i in range(self.total)
            if 0 <= self.place(i) + step < self.size
        ]
        return lax.ppermute(value, self.name, pairs)

    def swap(self, value, mask):
        pairs = [
            (i, i + ((self.place(i) ^ mask) - self.place(i)) * self.stride)
            for i in range(self.total)
        ]
        return lax.ppermute(value, self.name, pairs)

    def cross(self, value):
        return self.turn(value, (0, 2, 1, 3))

    def ends(self, value):
        return self.turn(value, (3, 1, 2, 0))

    def turn(self, value, order):
        pairs = [
            (i, i + (order[self.place(i)] - self.place(i)) * self.stride) for i in range(self.total)
        ]
        return lax.ppermute(value, self.name, pairs)

    def gather(self, pieces):
        return [pieces] + [[self.swap(p, m) for p in pieces] for m in range(1, self.size)]


def tick(*groups):
    sizes = [len(g) for g in groups]
    flat = lax.optimization_barrier(tuple(v for g in groups for v in g))
    out, at = [], 0
    for size in sizes:
        out.append(list(flat[at : at + size]))
        at += size
    return out


def local(body, outs, *operands, scratch=(), paced=CHEAP, left=0):
    vmem = pl.BlockSpec(memory_space=pltpu.VMEM)
    stay = pl.BlockSpec(memory_space=pltpu.HBM)
    return pl.pallas_call(
        body,
        out_shape=[jax.ShapeDtypeStruct(shape, kind) for shape, kind in outs],
        in_specs=[pl.BlockSpec(memory_space=pltpu.SMEM)] + [stay] * left
        + [vmem] * (len(operands) - 1 - left),
        out_specs=[vmem] * len(outs),
        scratch_shapes=list(scratch),
        cost_estimate=paced,
        compiler_params=pltpu.CompilerParams(vmem_limit_bytes=12 << 20),
    )(*operands)


def mlp_part(at, pieces, downs, shape, first=0, sofar=None):
    ny, nc, rows = shape
    ways, halves = len(pieces[0]), len(pieces)
    flat = [p for half in pieces for p in half]
    total = ny * nc * rows
    depth = pieces[0][0].shape[1]
    block = downs[0].shape[1]
    before = list(sofar or ())

    def body(at_ref, *refs):
        lhs, refs = refs[: ways * halves], refs[ways * halves :]
        d0, d1 = refs[:2]
        adds, (mine, theirs, taken, sems) = refs[2:-4], refs[-4:]
        inner = (at_ref[0] == 1) | (at_ref[0] == 2)

        def fetch(h, way):
            cols = pl.ds(h * depth, depth)
            return pltpu.make_async_copy(lhs[ways * h + way], taken.at[:, cols], sems.at[h])

        for h in range(halves):
            if ways == 1:
                fetch(h, 0).start()
                continue

            @pl.when(inner)
            def _():
                fetch(h, 0).start()

            @pl.when(jnp.logical_not(inner))
            def _():
                fetch(h, 1).start()

        for h in range(halves):
            fetch(h, 0).wait()

        here = at_ref[3] == 0
        deep = slice(first * depth, (first + halves) * depth)
        for j, down in enumerate((d0, d1)):

            @pl.loop(0, block // TILE)
            def _(t):
                part = jnp.dot(
                    taken[...],
                    down[deep, pl.ds(pl.multiple_of(t * TILE, TILE), TILE)],
                    preferred_element_type=F32,
                )
                cols = pl.ds(pl.multiple_of(j * block + t * TILE, TILE), TILE)
                for i in range(ny):
                    to = slice(i * rows, (i + 1) * rows)
                    one = part[(2 * i) * rows : (2 * i + 1) * rows]
                    two = part[(2 * i + 1) * rows : (2 * i + 2) * rows]
                    own, far = jnp.where(here, one, two), jnp.where(here, two, one)
                    if adds:
                        own, far = own + adds[0][to, cols], far + adds[1][to, cols]
                    mine[to, cols] = own
                    theirs[to, cols] = far

    out = ((ny * rows, 2 * block), F32)
    return local(
        body, [out, out], at, *flat, *downs, *before,
        scratch=[pltpu.VMEM((total, halves * depth), BF16), pltpu.SemaphoreType.DMA((halves,))],
        paced=SOME, left=len(flat),
    )


def core_add(at, mine, theirs, sent=F32):
    rows, cols = mine.shape[0] // 2, mine.shape[1]

    def body(at_ref, mine_ref, theirs_ref, keep, send):
        first = at_ref[2] == 0
        one = mine_ref[:rows] + theirs_ref[:rows]
        two = mine_ref[rows:] + theirs_ref[rows:]
        keep[...] = jnp.where(first, one, two)
        send[...] = jnp.where(first, two, one).astype(sent)

    return local(body, [((rows, cols), F32), ((rows, cols), sent)], at, mine, theirs)


def norm_part(at, keep, came, others, stream, gain):
    rows, cols = keep.shape
    block = cols // 2

    def body(at_ref, keep_ref, came_ref, q1, q2, q3, stream_ref, gain_ref, near, far, resid):
        zat, xat = at_ref[0], at_ref[1]
        square = jnp.zeros((rows, 1), F32)
        starts = []
        for m, ref in enumerate((None, q1, q2, q3)):
            for k in range(2):
                start = pl.multiple_of(((zat ^ m) * 2 + (xat ^ k)) * block, block)
                starts.append(start)
                here = slice(k * block, (k + 1) * block)
                if m == 0:
                    add = keep_ref[:, here] + came_ref[:, here]
                else:
                    add = ref[:, here]
                value = stream_ref[:, pl.ds(start, block)].astype(F32) + add
                square = square + jnp.sum(value * value, axis=-1, keepdims=True)
                at = (2 * m + k) * block
                resid[:, at : at + block] = value
        scale = lax.rsqrt(square / (8 * block) + 1e-06)
        for m, (ref, half) in enumerate(((near, 0), (far, 0), (far, 1), (near, 1))):
            for k in range(2):
                at = (2 * m + k) * block
                row = gain_ref[:, pl.ds(starts[2 * m + k], block)].astype(F32)
                to = (2 * half + k) * block
                ref[:, to : to + block] = (resid[:, at : at + block] * scale * row).astype(BF16)

    out = ((rows, 4 * block), BF16)
    return local(
        body, [out, out], at, keep, came, *others, stream, gain,
        scratch=[pltpu.VMEM((rows, 8 * block), F32)],
    )


def kv_part(at, rows, wk, wv, paced=CHEAP):
    count, width = rows[0].shape
    depth, cols = wk[0].shape
    pieces, parts = len(rows), len(wk) + len(wv)
    weights = [*wk, *wv]
    total = pieces * count

    def body(at_ref, *refs):
        out, stack, held, sems = refs[parts + pieces :]
        copies = [
            pltpu.make_async_copy(
                refs[parts + i], stack.at[pl.ds(i * count, count)], sems.at[parts + i]
            )
            for i in range(pieces)
        ]
        loads = [pltpu.make_async_copy(refs[p], held.at[p], sems.at[p]) for p in range(parts)]
        for copy in copies + loads:
            copy.start()
        for copy in copies:
            copy.wait()
        for p, load in enumerate(loads):
            load.wait()
            m = p % len(wk)
            to = slice(0, total) if p < len(wk) else slice(total, 2 * total)
            for t in range(cols // TILE):
                here = slice(t * TILE, (t + 1) * TILE)
                part = jnp.dot(
                    stack[:, m * depth : (m + 1) * depth],
                    held[p, :, here],
                    preferred_element_type=F32,
                )
                out[to, here] = part if m == 0 else out[to, here] + part

    return local(
        body, [((2 * total, cols), F32)], at, *weights, *rows,
        scratch=[
            pltpu.VMEM((total, width), BF16),
            pltpu.VMEM((parts, depth, cols), BF16),
            pltpu.SemaphoreType.DMA((parts + pieces,)),
        ],
        left=parts + pieces, paced=paced,
    )[0]


def softmax_part(at, own, came, queries, visible):
    total, cols = own.shape[0] // 2, own.shape[1]
    half = total // 2
    dec = queries.shape[0]
    heads = cols // HD

    def body(at_ref, own_ref, one, two, query, seen, out, keys):
        keys[:half] = (own_ref[:half] + one[:half]).astype(BF16)
        keys[half:] = (own_ref[half:total] + two[:half]).astype(BF16)
        for h in range(heads):
            here = slice(h * HD, (h + 1) * HD)
            scores = lax.dot_general(
                query[:, here], keys[:, here], (((1,), (1,)), ((), ())),
                preferred_element_type=F32,
            ) / math.sqrt(HD)
            scores = jnp.where(seen[...] > 0, scores, -jnp.inf)
            expo = jnp.exp(scores - jnp.max(scores, axis=-1, keepdims=True))
            weight = expo / jnp.sum(expo, axis=-1, keepdims=True)
            out[h * dec : (h + 1) * dec] = weight.astype(BF16)

    return local(
        body, [((heads * dec, total), BF16)], at, own, *came, queries, visible,
        scratch=[pltpu.VMEM((total, cols), BF16)], paced=CHEAP,
    )[0]


def out_part(at, own, came, weights, out_proj):
    total, cols = own.shape[0] // 2, own.shape[1]
    half = total // 2
    heads = cols // HD
    dec = weights.shape[0] // heads
    rows = dec // 4
    width = out_proj.shape[1]
    wide = 512

    def body(at_ref, own_ref, one, two, weight, proj, mine, theirs, values, attended, order):
        values[:half] = (own_ref[total : total + half] + one[half:]).astype(BF16)
        values[half:] = (own_ref[total + half :] + two[half:]).astype(BF16)
        live = lax.broadcasted_iota(jnp.int32, (dec, HD), 0) < dec - at_ref[5]
        for h in range(heads):
            here = slice(h * HD, (h + 1) * HD)
            value = jnp.dot(
                weight[h * dec : (h + 1) * dec], values[:, here], preferred_element_type=F32
            )
            attended[:, here] = jnp.where(live, value, 0.0).astype(BF16)
        first = at_ref[3] == 0
        for i in range(2):
            a = attended[(2 * i) * rows : (2 * i + 1) * rows]
            b = attended[(2 * i + 1) * rows : (2 * i + 2) * rows]
            order[i * rows : (i + 1) * rows] = jnp.where(first, a, b)
            order[(2 + i) * rows : (3 + i) * rows] = jnp.where(first, b, a)

        for t in range(width // wide):
            here = slice(t * wide, (t + 1) * wide)
            part = jnp.dot(order[...], proj[:, here], preferred_element_type=F32)
            mine[:, here] = part[: 2 * rows]
            theirs[:, here] = part[2 * rows :]

    return local(
        body, [((2 * rows, width), F32)] * 2, at, own, *came, weights, out_proj,
        scratch=[
            pltpu.VMEM((total, cols), BF16),
            pltpu.VMEM((dec, cols), BF16),
            pltpu.VMEM((dec, cols), BF16),
        ],
    )


def woven(z, x, y, c, hidden, down, kv, stream, gain, rows, query, out_proj, visible, pad):
    E, O, X, Y = (lambda v: z.swap(v, 1)), z.cross, (lambda v: x.swap(v, 1)), (lambda v: y.swap(v, 1))
    C = lambda v: c.swap(v, 1)
    at = jnp.stack([z.at, x.at, y.at, c.at, z.at, pad]).astype(jnp.int32)
    inner = (z.at == 1) | (z.at == 2)
    half = hidden.shape[1] // 2
    ha, hb = hidden[:, :half], hidden[:, half:]
    k, v = kv
    product = lambda pieces, xd, **more: mlp_part(at, pieces, (down, xd), (2, 2, rows), **more)

    e1a, o1a, xd = E(ha), O(ha), X(down)
    e1b, o1b = E(hb), O(hb)
    e2a, o2a = E(o1a), O(e1a)
    e2b, o2b = E(o1b), O(e1b)
    e3a, e3b = E(o2a), E(o2b)

    (o2a,), (k, v) = tick((o2a,), (k, v))
    ok, ov, xk0 = O(k), O(v), X(k)
    (e2a, o2a, e2b, o2b, xd), (k, v) = tick((e2a, o2a, e2b, o2b, xd), (k, v))
    m1, h1 = product(((e1a,), (e1b,)), xd)
    m2, h2 = product(((o2a, e2a), (o2b, e2b)), xd)
    m0, h0 = product(((ha,), (hb,)), xd)
    part3 = product(((o1a, e3a),), xd)

    done = (m1, h1, m2, h2, m0, h0, e3b, ok, ov, xk0, *part3)
    (m1, h1, m2, h2, m0, h0, e3b, ok, ov, xk0, *part3), (k, v) = tick(done, (k, v))
    fk, fv = z.ends(k), z.ends(v)
    xv0 = X(v)
    h1, h2, h0 = C(h1), C(h2), C(h0)
    m3, h3 = product(((o1b, e3b),), xd, first=1, sofar=part3)

    (h1, h2, h0, m3, h3), = tick((h1, h2, h0, m3, h3))
    h3 = C(h3)
    k2, s2 = core_add(at, m2, h2)
    s2 = Y(s2)
    k1, s1 = core_add(at, m1, h1)
    k0, s0 = core_add(at, m0, h0)

    (h3, k1, s1, k0, s0), = tick((h3, k1, s1, k0, s0))
    k3, s3 = core_add(at, m3, h3)
    s3 = Y(s3)

    (s2,), (s1, s0) = tick((s2,), (s1, s0))
    q2 = z.swap(k2 + s2, 2)
    s1 = Y(s1)

    (s3, fk, xv0), (s0, v, ov) = tick((s3, fk, xv0), (s0, v, ov))
    q3 = z.swap(k3 + s3, 3)
    s0 = Y(s0)
    kk = jnp.where(inner, ok, fk)
    xkk = X(kk)

    (s1,), = tick((s1,))
    q1 = z.swap(k1 + s1, 1)

    vv = jnp.where(inner, ov, fv)
    xvv = X(vv)
    (q1, q2, q3, s0, xkk), = tick((q1, q2, q3, s0, xkk))
    mine, other = norm_part(at, k0, s0, (q1, q2, q3), stream, gain)
    near, far = E(other), Y(mine)
    (near, far, xvv), = tick((near, far, xvv))
    nearfar = Y(near)
    near2, mine2, far2 = C(near), C(mine), C(far)
    (near2,), = tick((near2,))
    wk, wv = (k, xk0, kk, xkk), (v, xv0, vv, xvv)
    sums1 = E(kv_part(at, (near, near2), wk, wv))
    nearfar2 = C(nearfar)
    sums2 = kv_part(at, (nearfar, nearfar2), wk, wv, cost(1))
    (sums1, sums2), own = tick((sums1, sums2), (mine, mine2, far, far2))
    came = sums1, E(sums2)
    sums = kv_part(at, own, wk, wv)
    weight = softmax_part(at, sums, came, query, visible)
    m, h = out_part(at, sums, came, weight, out_proj)
    keep, send = core_add(at, m, C(h), BF16)
    return (keep + Y(send).astype(F32)).astype(BF16)


def on_device(
    mlp_hidden, encoder_stream, down_proj, final_gain, kv_proj, queries, out_proj, enc_len, dec_pad
):
    seq, dp = lax.axis_size("seq"), lax.axis_size("dp")
    nx = 1 << ((dp.bit_length() - 1) // 2)
    nz = dp // nx
    nc = 2
    ny = seq // nc
    z = Line("dp", dp, nz, nx)
    x = Line("dp", dp, nx, 1)
    y = Line("seq", seq, ny, nc)
    c = Line("seq", seq, nc, 1)

    hidden = mlp_hidden[0]
    enc_total, depth = hidden.shape
    rows = enc_total // seq
    block = down_proj.shape[1]
    width = block * dp
    dot = lambda a, b: jnp.dot(a, b, preferred_element_type=jnp.float32)

    half = depth // 2
    halves = [hidden[:, :half], hidden[:, half:]]
    downs = [down_proj[:half], down_proj[half:]]
    kv_local = [kv_proj[:, 0], kv_proj[:, 1]]

    def seq_core(part):
        part = part.reshape(ny, nc, rows, nx * block)
        pick = lambda i: lax.dynamic_index_in_dim(part, i, 1, keepdims=False)
        return pick(c.at), c.swap(pick(1 - c.at), 1)

    def seq_y(mine, theirs):
        part = mine + theirs
        total = lax.dynamic_index_in_dim(part, y.at, 0, keepdims=False)
        others = [
            y.swap(lax.dynamic_index_in_dim(part, y.at ^ k, 0, keepdims=False), k)
            for k in range(1, ny)
        ]
        return [total] + others

    stream = encoder_stream[0]
    gain = final_gain.astype(jnp.float32)

    def norm(summed):
        resid, gains = [], []
        for m in range(nz):
            for k in range(nx):
                start = ((z.at ^ m) * nx + (x.at ^ k)) * block
                piece = lax.dynamic_slice_in_dim(stream, start, block, 1).astype(jnp.float32)
                resid.append(piece + summed[m][:, k * block : (k + 1) * block])
                gains.append(lax.dynamic_slice_in_dim(gain, start, block, 0))
        resid = jnp.concatenate(resid, axis=1)
        gains = jnp.concatenate(gains, axis=0)
        spread = jnp.sum(resid * resid, axis=-1, keepdims=True) / width
        return (resid * lax.rsqrt(spread + 1e-06) * gains).astype(jnp.bfloat16)

    places = []
    for k in range(ny):
        for j in range(nc):
            start = ((y.at ^ k) * nc + (c.at ^ j)) * rows
            places.append(start + jnp.arange(rows, dtype=jnp.int32))
    visible = jnp.concatenate(places) < enc_len[0]

    if (nz, nx, ny) == (4, 2, 2):
        return woven(
            z, x, y, c, hidden, down_proj, kv_local, stream, final_gain[None], rows, queries[0],
            out_proj, visible.astype(jnp.int32)[None], dec_pad[0],
        )[None]
    else:
        hidden_slots = z.gather(halves)
        down_slots = x.gather(downs)
        kv_slots = [x.gather(slot) for slot in z.gather(kv_local)]
        weights = [jnp.concatenate([s[p] for s in down_slots], axis=1) for p in range(2)]
        summed = []
        for m in range(nz):
            part = dot(hidden_slots[m][0], weights[0]) + dot(hidden_slots[m][1], weights[1])
            total = sum(seq_y(*seq_core(part)))
            summed.append(total if m == 0 else z.swap(total, m))
        encoded = []
        for (far,) in y.gather([norm(summed)]):
            encoded += [far, c.swap(far, 1)]
        encoded = jnp.concatenate(encoded, axis=0)
        keys = values = 0.0
        for m in range(nz):
            for k in range(nx):
                at = (m * nx + k) * block
                piece = encoded[:, at : at + block]
                keys = keys + dot(piece, kv_slots[m][k][0])
                values = values + dot(piece, kv_slots[m][k][1])
    keys = keys.astype(jnp.bfloat16)
    values = values.astype(jnp.bfloat16)

    heads_here = queries.shape[2] // HD
    dec_rows = queries.shape[1]
    attended = []
    for h in range(heads_here):
        cols = slice(h * HD, (h + 1) * HD)
        scores = lax.dot_general(
            queries[0][:, cols], keys[:, cols], (((1,), (1,)), ((), ())),
            preferred_element_type=jnp.float32,
        ) / math.sqrt(HD)
        scores = jnp.where(visible[None, :], scores, -jnp.inf)
        expo = jnp.exp(scores - jnp.max(scores, axis=-1, keepdims=True))
        attention = (expo / jnp.sum(expo, axis=-1, keepdims=True)).astype(jnp.bfloat16)
        attended.append(dot(attention, values[:, cols]).astype(jnp.bfloat16))
    attended = jnp.concatenate(attended, axis=1)
    row_live = jnp.arange(dec_rows, dtype=jnp.int32) < dec_rows - dec_pad[0]
    attended = jnp.where(row_live[:, None], attended, jnp.zeros_like(attended))

    out_rows = dec_rows // seq
    att = attended.reshape(ny, nc, out_rows, heads_here * HD)
    pick = lambda i: lax.dynamic_index_in_dim(att, i, 1, keepdims=False).reshape(
        ny * out_rows, heads_here * HD
    )
    part = dot(pick(c.at), out_proj) + c.swap(dot(pick(1 - c.at), out_proj), 1)
    part = part.reshape(ny, out_rows, width)
    total = lax.dynamic_index_in_dim(part, y.at, 0, keepdims=False)
    for k in range(1, ny):
        other = lax.dynamic_index_in_dim(part, y.at ^ k, 0, keepdims=False).astype(BF16)
        total = total + y.swap(other, k).astype(F32)
    return total.astype(jnp.bfloat16)[None]


def solution(mesh):
    placed = (
        P("dp", None, "seq"),
        P("dp", "seq", None),
        P("seq", "dp"),
        P(),
        P("dp", None, "seq"),
        P("dp", None, "seq"),
        P("seq", None),
        P("dp"),
        P("dp"),
    )
    return jax.shard_map(
        on_device, mesh=mesh, in_specs=placed, out_specs=P("dp", "seq", None), check_vma=False
    )
```

```python
import math

import jax
import jax.numpy as jnp
from jax import lax
from jax.experimental import pallas as pl
from jax.experimental.pallas import tpu as pltpu
from jax.sharding import PartitionSpec as P

HD = 256
TILE = 256
F32, BF16 = jnp.float32, jnp.bfloat16


def cost(us):
    return pl.CostEstimate(flops=1, bytes_accessed=int(1 + us * 3_500_000), transcendentals=0)


CHEAP, SOME = cost(0), cost(0.5)


class Line:
    def __init__(self, name, total, size, stride):
        self.name, self.total, self.size, self.stride = name, total, size, stride
        self.at = (lax.axis_index(name) // stride) % size

    def place(self, index):
        return (index // self.stride) % self.size

    def shift(self, value, step):
        pairs = [
            (i, i + step * self.stride)
            for i in range(self.total)
            if 0 <= self.place(i) + step < self.size
        ]
        return lax.ppermute(value, self.name, pairs)

    def swap(self, value, mask):
        pairs = [
            (i, i + ((self.place(i) ^ mask) - self.place(i)) * self.stride)
            for i in range(self.total)
        ]
        return lax.ppermute(value, self.name, pairs)

    def cross(self, value):
        return self.turn(value, (0, 2, 1, 3))

    def ends(self, value):
        return self.turn(value, (3, 1, 2, 0))

    def turn(self, value, order):
        pairs = [
            (i, i + (order[self.place(i)] - self.place(i)) * self.stride) for i in range(self.total)
        ]
        return lax.ppermute(value, self.name, pairs)

    def gather(self, pieces):
        return [pieces] + [[self.swap(p, m) for p in pieces] for m in range(1, self.size)]


def tick(*groups):
    sizes = [len(g) for g in groups]
    flat = lax.optimization_barrier(tuple(v for g in groups for v in g))
    out, at = [], 0
    for size in sizes:
        out.append(list(flat[at : at + size]))
        at += size
    return out


def local(body, outs, *operands, scratch=(), paced=CHEAP, left=0):
    vmem = pl.BlockSpec(memory_space=pltpu.VMEM)
    stay = pl.BlockSpec(memory_space=pltpu.HBM)
    return pl.pallas_call(
        body,
        out_shape=[jax.ShapeDtypeStruct(shape, kind) for shape, kind in outs],
        in_specs=[pl.BlockSpec(memory_space=pltpu.SMEM)] + [stay] * left
        + [vmem] * (len(operands) - 1 - left),
        out_specs=[vmem] * len(outs),
        scratch_shapes=list(scratch),
        cost_estimate=paced,
        compiler_params=pltpu.CompilerParams(vmem_limit_bytes=12 << 20),
    )(*operands)


def mlp_part(at, pieces, downs, shape, first=0, sofar=None):
    ny, nc, rows = shape
    ways, halves = len(pieces[0]), len(pieces)
    flat = [p for half in pieces for p in half]
    total = ny * nc * rows
    depth = pieces[0][0].shape[1]
    block = downs[0].shape[1]
    before = list(sofar or ())

    def body(at_ref, *refs):
        lhs, refs = refs[: ways * halves], refs[ways * halves :]
        d0, d1 = refs[:2]
        adds, (mine, theirs, taken, sems) = refs[2:-4], refs[-4:]
        inner = (at_ref[0] == 1) | (at_ref[0] == 2)

        def fetch(h, way):
            cols = pl.ds(h * depth, depth)
            return pltpu.make_async_copy(lhs[ways * h + way], taken.at[:, cols], sems.at[h])

        for h in range(halves):
            if ways == 1:
                fetch(h, 0).start()
                continue

            @pl.when(inner)
            def _():
                fetch(h, 0).start()

            @pl.when(jnp.logical_not(inner))
            def _():
                fetch(h, 1).start()

        for h in range(halves):
            fetch(h, 0).wait()

        here = at_ref[3] == 0
        deep = slice(first * depth, (first + halves) * depth)
        for j, down in enumerate((d0, d1)):

            @pl.loop(0, block // TILE)
            def _(t):
                part = jnp.dot(
                    taken[...],
                    down[deep, pl.ds(pl.multiple_of(t * TILE, TILE), TILE)],
                    preferred_element_type=F32,
                )
                cols = pl.ds(pl.multiple_of(j * block + t * TILE, TILE), TILE)
                for i in range(ny):
                    to = slice(i * rows, (i + 1) * rows)
                    one = part[(2 * i) * rows : (2 * i + 1) * rows]
                    two = part[(2 * i + 1) * rows : (2 * i + 2) * rows]
                    own, far = jnp.where(here, one, two), jnp.where(here, two, one)
                    if adds:
                        own, far = own + adds[0][to, cols], far + adds[1][to, cols]
                    mine[to, cols] = own
                    theirs[to, cols] = far

    out = ((ny * rows, 2 * block), F32)
    return local(
        body, [out, out], at, *flat, *downs, *before,
        scratch=[pltpu.VMEM((total, halves * depth), BF16), pltpu.SemaphoreType.DMA((halves,))],
        paced=SOME, left=len(flat),
    )


def core_add(at, mine, theirs, sent=F32):
    rows, cols = mine.shape[0] // 2, mine.shape[1]
    if not isinstance(theirs, (list, tuple)):
        theirs = [theirs[:rows], theirs[rows:]]

    def body(at_ref, mine_ref, low, high, keep, send):
        first = at_ref[2] == 0
        one = mine_ref[:rows] + low[...]
        two = mine_ref[rows:] + high[...]
        keep[...] = jnp.where(first, one, two)
        send[...] = jnp.where(first, two, one).astype(sent)

    return local(body, [((rows, cols), F32), ((rows, cols), sent)], at, mine, *theirs)


def norm_part(at, keep, came, others, stream, gain):
    rows, cols = keep.shape
    block = cols // 2

    def body(at_ref, keep_ref, came_ref, q1, q2, q3, stream_ref, gain_ref, near, far, resid):
        zat, xat = at_ref[0], at_ref[1]
        square = jnp.zeros((rows, 1), F32)
        starts = []
        for m, ref in enumerate((None, q1, q2, q3)):
            for k in range(2):
                start = pl.multiple_of(((zat ^ m) * 2 + (xat ^ k)) * block, block)
                starts.append(start)
                here = slice(k * block, (k + 1) * block)
                if m == 0:
                    add = keep_ref[:, here] + came_ref[:, here]
                else:
                    add = ref[:, here]
                value = stream_ref[:, pl.ds(start, block)].astype(F32) + add
                square = square + jnp.sum(value * value, axis=-1, keepdims=True)
                at = (2 * m + k) * block
                resid[:, at : at + block] = value
        scale = lax.rsqrt(square / (8 * block) + 1e-06)
        for m, (ref, half) in enumerate(((near, 0), (far, 0), (far, 1), (near, 1))):
            for k in range(2):
                at = (2 * m + k) * block
                row = gain_ref[:, pl.ds(starts[2 * m + k], block)].astype(F32)
                to = (2 * half + k) * block
                ref[:, to : to + block] = (resid[:, at : at + block] * scale * row).astype(BF16)

    out = ((rows, 4 * block), BF16)
    return local(
        body, [out, out], at, keep, came, *others, stream, gain,
        scratch=[pltpu.VMEM((rows, 8 * block), F32)],
    )


def kv_part(at, rows, wk, wv, paced=CHEAP):
    count, width = rows[0].shape
    depth, cols = wk[0].shape
    pieces, parts = len(rows), len(wk) + len(wv)
    weights = [*wk, *wv]
    total = pieces * count

    def body(at_ref, *refs):
        out, stack, held, sems = refs[parts + pieces :]
        copies = [
            pltpu.make_async_copy(
                refs[parts + i], stack.at[pl.ds(i * count, count)], sems.at[parts + i]
            )
            for i in range(pieces)
        ]
        loads = [pltpu.make_async_copy(refs[p], held.at[p], sems.at[p]) for p in range(parts)]
        for copy in copies + loads:
            copy.start()
        for copy in copies:
            copy.wait()
        for p, load in enumerate(loads):
            load.wait()
            m = p % len(wk)
            to = slice(0, total) if p < len(wk) else slice(total, 2 * total)
            for t in range(cols // TILE):
                here = slice(t * TILE, (t + 1) * TILE)
                part = jnp.dot(
                    stack[:, m * depth : (m + 1) * depth],
                    held[p, :, here],
                    preferred_element_type=F32,
                )
                out[to, here] = part if m == 0 else out[to, here] + part

    return local(
        body, [((2 * total, cols), F32)], at, *weights, *rows,
        scratch=[
            pltpu.VMEM((total, width), BF16),
            pltpu.VMEM((parts, depth, cols), BF16),
            pltpu.SemaphoreType.DMA((parts + pieces,)),
        ],
        left=parts + pieces, paced=paced,
    )[0]


def softmax_part(at, own, came, queries, visible):
    total, cols = own.shape[0] // 2, own.shape[1]
    half = total // 2
    dec = queries.shape[0]
    heads = cols // HD

    def body(at_ref, own_ref, one, two, query, seen, out, keys):
        keys[:half] = (own_ref[:half] + one[:half]).astype(BF16)
        keys[half:] = (own_ref[half:total] + two[:half]).astype(BF16)
        for h in range(heads):
            here = slice(h * HD, (h + 1) * HD)
            scores = lax.dot_general(
                query[:, here], keys[:, here], (((1,), (1,)), ((), ())),
                preferred_element_type=F32,
            ) / math.sqrt(HD)
            scores = jnp.where(seen[...] > 0, scores, -jnp.inf)
            expo = jnp.exp(scores - jnp.max(scores, axis=-1, keepdims=True))
            weight = expo / jnp.sum(expo, axis=-1, keepdims=True)
            out[h * dec : (h + 1) * dec] = weight.astype(BF16)

    return local(
        body, [((heads * dec, total), BF16)], at, own, *came, queries, visible,
        scratch=[pltpu.VMEM((total, cols), BF16)], paced=CHEAP,
    )[0]


def out_part(at, own, came, weights, out_proj):
    total, cols = own.shape[0] // 2, own.shape[1]
    half = total // 2
    heads = cols // HD
    dec = weights.shape[0] // heads
    rows = dec // 4
    width = out_proj.shape[1]
    wide = 512

    def body(at_ref, own_ref, one, two, weight, proj, mine, theirs, values, attended, order):
        values[:half] = (own_ref[total : total + half] + one[half:]).astype(BF16)
        values[half:] = (own_ref[total + half :] + two[half:]).astype(BF16)
        live = lax.broadcasted_iota(jnp.int32, (dec, HD), 0) < dec - at_ref[5]
        for h in range(heads):
            here = slice(h * HD, (h + 1) * HD)
            value = jnp.dot(
                weight[h * dec : (h + 1) * dec], values[:, here], preferred_element_type=F32
            )
            attended[:, here] = jnp.where(live, value, 0.0).astype(BF16)
        first = at_ref[3] == 0
        for i in range(2):
            a = attended[(2 * i) * rows : (2 * i + 1) * rows]
            b = attended[(2 * i + 1) * rows : (2 * i + 2) * rows]
            order[i * rows : (i + 1) * rows] = jnp.where(first, a, b)
            order[(2 + i) * rows : (3 + i) * rows] = jnp.where(first, b, a)

        for t in range(width // wide):
            here = slice(t * wide, (t + 1) * wide)
            part = jnp.dot(order[...], proj[:, here], preferred_element_type=F32)
            mine[:, here] = part[: 2 * rows]
            theirs[:, here] = part[2 * rows :]

    return local(
        body, [((2 * rows, width), F32)] * 2, at, own, *came, weights, out_proj,
        scratch=[
            pltpu.VMEM((total, cols), BF16),
            pltpu.VMEM((dec, cols), BF16),
            pltpu.VMEM((dec, cols), BF16),
        ],
    )


def woven(z, x, y, c, hidden, down, kv, stream, gain, rows, query, out_proj, visible, pad):
    E, O, X, Y = (lambda v: z.swap(v, 1)), z.cross, (lambda v: x.swap(v, 1)), (lambda v: y.swap(v, 1))
    C = lambda v: c.swap(v, 1)
    at = jnp.stack([z.at, x.at, y.at, c.at, z.at, pad]).astype(jnp.int32)
    inner = (z.at == 1) | (z.at == 2)
    half = hidden.shape[1] // 2
    ha, hb = hidden[:, :half], hidden[:, half:]
    k, v = kv
    product = lambda pieces, xd, **more: mlp_part(at, pieces, (down, xd), (2, 2, rows), **more)

    e1a, o1a, xd = E(ha), O(ha), X(down)
    e1b, o1b = E(hb), O(hb)
    e2a, o2a = E(o1a), O(e1a)
    e2b, o2b = E(o1b), O(e1b)
    e3a, e3b = E(o2a), E(o2b)

    (o2a,), (k, v) = tick((o2a,), (k, v))
    ok, ov, xk0 = O(k), O(v), X(k)
    (e2a, o2a, e2b, o2b, xd), (k, v) = tick((e2a, o2a, e2b, o2b, xd), (k, v))
    fk = z.ends(k)
    m1, h1 = product(((e1a,), (e1b,)), xd)
    m2, h2 = product(((o2a, e2a), (o2b, e2b)), xd)
    m0, h0 = product(((ha,), (hb,)), xd)
    part3 = product(((o1a, e3a),), xd)

    done = (m1, h1, m2, h2, m0, h0, e3b, ok, ov, xk0, *part3)
    (m1, h1, m2, h2, m0, h0, e3b, ok, ov, xk0, *part3), (k, v) = tick(done, (k, v))
    fv = z.ends(v)
    xv0 = X(v)
    m3, h3 = product(((o1b, e3b),), xd, first=1, sofar=part3)

    sides = [C(part) for h in (h1, h2, h0) for part in jnp.split(h, 2, axis=0)]
    sides, (m3, h3, fk) = tick(sides, (m3, h3, fk))
    h1, h2, h0 = sides[:2], sides[2:4], sides[4:]
    h3 = [C(part) for part in jnp.split(h3, 2, axis=0)]
    k2, s2 = core_add(at, m2, h2)
    s2 = Y(s2)
    k1, s1 = core_add(at, m1, h1)
    k0, s0 = core_add(at, m0, h0)

    (h3, k1, s1, k0, s0), = tick((h3, k1, s1, k0, s0))
    k3, s3 = core_add(at, m3, h3)
    s3 = Y(s3)

    (s2,), (s1, s0) = tick((s2,), (s1, s0))
    q2 = z.swap(k2 + s2, 2)
    s1 = Y(s1)

    (s3, fk, xv0), (s0, v, ov) = tick((s3, fk, xv0), (s0, v, ov))
    q3 = z.swap(k3 + s3, 3)
    s0 = Y(s0)
    kk = jnp.where(inner, ok, fk)
    xkk = X(kk)

    (s1, fv), = tick((s1, fv))
    q1 = z.swap(k1 + s1, 1)

    vv = jnp.where(inner, ov, fv)
    xvv = X(vv)
    (q1, q2, q3, s0, xkk), = tick((q1, q2, q3, s0, xkk))
    mine, other = norm_part(at, k0, s0, (q1, q2, q3), stream, gain)
    near, far = E(other), Y(mine)
    (near, far, xvv), = tick((near, far, xvv))
    nearfar = Y(near)
    near2, mine2, far2 = C(near), C(mine), C(far)
    (near2,), = tick((near2,))
    wk, wv = (k, xk0, kk, xkk), (v, xv0, vv, xvv)
    sums1 = E(kv_part(at, (near, near2), wk, wv))
    nearfar2 = C(nearfar)
    sums2 = kv_part(at, (nearfar, nearfar2), wk, wv, cost(1))
    (sums1, sums2), own = tick((sums1, sums2), (mine, mine2, far, far2))
    came = sums1, E(sums2)
    sums = kv_part(at, own, wk, wv)
    weight = softmax_part(at, sums, came, query, visible)
    m, h = out_part(at, sums, came, weight, out_proj)
    keep, send = core_add(at, m, [C(part) for part in jnp.split(h, 2, axis=0)], BF16)
    return (keep + Y(send).astype(F32)).astype(BF16)


def on_device(
    mlp_hidden, encoder_stream, down_proj, final_gain, kv_proj, queries, out_proj, enc_len, dec_pad
):
    seq, dp = lax.axis_size("seq"), lax.axis_size("dp")
    nx = 1 << ((dp.bit_length() - 1) // 2)
    nz = dp // nx
    nc = 2
    ny = seq // nc
    z = Line("dp", dp, nz, nx)
    x = Line("dp", dp, nx, 1)
    y = Line("seq", seq, ny, nc)
    c = Line("seq", seq, nc, 1)

    hidden = mlp_hidden[0]
    enc_total, depth = hidden.shape
    rows = enc_total // seq
    block = down_proj.shape[1]
    width = block * dp
    dot = lambda a, b: jnp.dot(a, b, preferred_element_type=jnp.float32)

    half = depth // 2
    halves = [hidden[:, :half], hidden[:, half:]]
    downs = [down_proj[:half], down_proj[half:]]
    kv_local = [kv_proj[:, 0], kv_proj[:, 1]]

    def seq_core(part):
        part = part.reshape(ny, nc, rows, nx * block)
        pick = lambda i: lax.dynamic_index_in_dim(part, i, 1, keepdims=False)
        return pick(c.at), c.swap(pick(1 - c.at), 1)

    def seq_y(mine, theirs):
        part = mine + theirs
        total = lax.dynamic_index_in_dim(part, y.at, 0, keepdims=False)
        others = [
            y.swap(lax.dynamic_index_in_dim(part, y.at ^ k, 0, keepdims=False), k)
            for k in range(1, ny)
        ]
        return [total] + others

    stream = encoder_stream[0]
    gain = final_gain.astype(jnp.float32)

    def norm(summed):
        resid, gains = [], []
        for m in range(nz):
            for k in range(nx):
                start = ((z.at ^ m) * nx + (x.at ^ k)) * block
                piece = lax.dynamic_slice_in_dim(stream, start, block, 1).astype(jnp.float32)
                resid.append(piece + summed[m][:, k * block : (k + 1) * block])
                gains.append(lax.dynamic_slice_in_dim(gain, start, block, 0))
        resid = jnp.concatenate(resid, axis=1)
        gains = jnp.concatenate(gains, axis=0)
        spread = jnp.sum(resid * resid, axis=-1, keepdims=True) / width
        return (resid * lax.rsqrt(spread + 1e-06) * gains).astype(jnp.bfloat16)

    places = []
    for k in range(ny):
        for j in range(nc):
            start = ((y.at ^ k) * nc + (c.at ^ j)) * rows
            places.append(start + jnp.arange(rows, dtype=jnp.int32))
    visible = jnp.concatenate(places) < enc_len[0]

    if (nz, nx, ny) == (4, 2, 2):
        return woven(
            z, x, y, c, hidden, down_proj, kv_local, stream, final_gain[None], rows, queries[0],
            out_proj, visible.astype(jnp.int32)[None], dec_pad[0],
        )[None]
    else:
        hidden_slots = z.gather(halves)
        down_slots = x.gather(downs)
        kv_slots = [x.gather(slot) for slot in z.gather(kv_local)]
        weights = [jnp.concatenate([s[p] for s in down_slots], axis=1) for p in range(2)]
        summed = []
        for m in range(nz):
            part = dot(hidden_slots[m][0], weights[0]) + dot(hidden_slots[m][1], weights[1])
            total = sum(seq_y(*seq_core(part)))
            summed.append(total if m == 0 else z.swap(total, m))
        encoded = []
        for (far,) in y.gather([norm(summed)]):
            encoded += [far, c.swap(far, 1)]
        encoded = jnp.concatenate(encoded, axis=0)
        keys = values = 0.0
        for m in range(nz):
            for k in range(nx):
                at = (m * nx + k) * block
                piece = encoded[:, at : at + block]
                keys = keys + dot(piece, kv_slots[m][k][0])
                values = values + dot(piece, kv_slots[m][k][1])
    keys = keys.astype(jnp.bfloat16)
    values = values.astype(jnp.bfloat16)

    heads_here = queries.shape[2] // HD
    dec_rows = queries.shape[1]
    attended = []
    for h in range(heads_here):
        cols = slice(h * HD, (h + 1) * HD)
        scores = lax.dot_general(
            queries[0][:, cols], keys[:, cols], (((1,), (1,)), ((), ())),
            preferred_element_type=jnp.float32,
        ) / math.sqrt(HD)
        scores = jnp.where(visible[None, :], scores, -jnp.inf)
        expo = jnp.exp(scores - jnp.max(scores, axis=-1, keepdims=True))
        attention = (expo / jnp.sum(expo, axis=-1, keepdims=True)).astype(jnp.bfloat16)
        attended.append(dot(attention, values[:, cols]).astype(jnp.bfloat16))
    attended = jnp.concatenate(attended, axis=1)
    row_live = jnp.arange(dec_rows, dtype=jnp.int32) < dec_rows - dec_pad[0]
    attended = jnp.where(row_live[:, None], attended, jnp.zeros_like(attended))

    out_rows = dec_rows // seq
    att = attended.reshape(ny, nc, out_rows, heads_here * HD)
    pick = lambda i: lax.dynamic_index_in_dim(att, i, 1, keepdims=False).reshape(
        ny * out_rows, heads_here * HD
    )
    part = dot(pick(c.at), out_proj) + c.swap(dot(pick(1 - c.at), out_proj), 1)
    part = part.reshape(ny, out_rows, width)
    total = lax.dynamic_index_in_dim(part, y.at, 0, keepdims=False)
    for k in range(1, ny):
        other = lax.dynamic_index_in_dim(part, y.at ^ k, 0, keepdims=False).astype(BF16)
        total = total + y.swap(other, k).astype(F32)
    return total.astype(jnp.bfloat16)[None]


def solution(mesh):
    placed = (
        P("dp", None, "seq"),
        P("dp", "seq", None),
        P("seq", "dp"),
        P(),
        P("dp", None, "seq"),
        P("dp", None, "seq"),
        P("seq", None),
        P("dp"),
        P("dp"),
    )
    return jax.shard_map(
        on_device, mesh=mesh, in_specs=placed, out_specs=P("dp", "seq", None), check_vma=False
    )
```
